32 devices in a mesh: seg: 4 (over y, x), grid: 8 (over z, core).
Axes of the slice: x: 2, y: 2, z: 4, core: 2. Of those that a mesh axis runs over, the one named last changes fastest.
Arguments:
- tangent: float32 [4, 3, 96, 256, 256], P('seg', None, 'grid'), may hold values from -6 to 6
- base_flow: bfloat16 [4, 3, 96, 256, 256], P('seg', None, 'grid'), may hold values from -4 to 4
- base_shear: bfloat16 [4, 3, 96, 256, 256], P('seg', None, 'grid'), may hold values from -4 to 4
- wall_derivative: float32 [96, 96], replicated, may hold values from -0.625 to 0.625
- implicit_inverse: float32 [3, 96, 96], replicated, may hold values from -1 to 1
- successor: int32 [4], replicated, may hold values from 0 to 3, as said below
- spanwise_shift: int32 [4], P('seg'), may hold values from 0 to 255
Outputs:
- jvp: float32 [4, 3, 96, 256, 256], P('seg', None, 'grid')
The draws below stay inside these ranges and needn't reach their ends.
Inputs may be any that keep to these rules, and one draw needn't show every extreme that they name: successor[s] = (s + k) mod 4 for one odd k shared by all segments, so the segments form one closed loop.
All inputs are finite; a program needn't handle non-finite values.
Results may differ from the reference program's by a relative error of at most 0.0003.
Values may be sent and summed in bfloat16 or wider, within the bound.
No kernel may reach another device: no remote copies, remote signals or barrier semaphores. Data moves between devices by JAX's collectives and lax.ppermute only.
A program may use at most 192 MiB of HBM per device.

```python
import math
import jax
import jax.numpy as jnp
from jax import lax

NX = 256
NY = 96
NZ = 256
STEPS = 1
SEGS = 4


def draw_implicit_inverse(key, part):
    key_diagonal, key_spread = jax.random.split(key)
    diagonal = jax.random.uniform(key_diagonal, (3, NY), jnp.float32, 0.6, 0.9)
    spread = 0.3 * jax.random.truncated_normal(key_spread, -4.0, 4.0, (3, NY, NY), jnp.float32)
    spread = spread * float(NY) ** (-0.5)
    identity = jnp.eye(NY, dtype=jnp.float32)
    return spread * (1.0 - identity) + identity * diagonal[:, :, None]


def draw_successor(key, part):
    stride = 2 * jax.random.randint(key, (), 0, max(SEGS // 2, 1)) + 1
    return ((jnp.arange(SEGS, dtype=jnp.int32) + stride) % SEGS).astype(jnp.int32)


def touch_ends(drawn, stream_key, smallest, top_value):
    extent = drawn.shape
    spot = [jax.random.randint(jax.random.fold_in(stream_key, axis), (), 0, extent[axis]) for axis in range(len(extent))]
    drawn = drawn.at[tuple(spot)].set(smallest)
    longest = extent.index(max(extent))
    spot[longest] = (spot[longest] + 1) % extent[longest]
    return drawn.at[tuple(spot)].set(top_value)


def levels(stream_key, shape, shards, low, largest):
    def one(dim, shards_of):
        steps = jax.random.uniform(jax.random.fold_in(jax.random.fold_in(stream_key, 6), dim), (shards_of,), jnp.float32, low / len(shards), largest / len(shards))
        return jnp.repeat(jnp.exp(steps), shape[dim] // shards_of).reshape((-1,) + (1,) * (len(shape) - dim - 1))

    gain = one(*shards[0])
    for cut in shards[1:]:
        gain = gain * one(*cut)
    return gain


def centred(key, dims, scale, most, shards=(), held_as=jnp.bfloat16):
    array = scale * jax.random.normal(key, dims, jnp.float32)
    if shards:
        array = array * levels(key, dims, shards, -0.22, 0.18)
    return jnp.clip(array, -most, most).astype(held_as)


def setup_inputs(seed: int = 0) -> dict:
    keys = jax.random.split(jax.random.key(seed), 8)
    return {
        "tangent": centred(keys[0], (SEGS, 3, NY, NX, NZ), 1.0, 6.0, ((0, 4), (2, 8)), jnp.float32),
        "base_flow": centred(keys[1], (SEGS, 3, NY, NX, NZ), 1.0, 4.0, ((0, 4), (2, 8))),
        "base_shear": centred(keys[2], (SEGS, 3, NY, NX, NZ), 1.0, 4.0, ((0, 4), (2, 8))),
        "wall_derivative": centred(keys[3], (NY, NY), NY ** -0.5, 0.625, (), jnp.float32),
        "implicit_inverse": draw_implicit_inverse(jax.random.fold_in(keys[7], 71), 0),
        "successor": draw_successor(jax.random.fold_in(keys[7], 71), 0),
        "spanwise_shift": touch_ends(jax.random.randint(keys[6], (SEGS,), 0, NZ), jax.random.fold_in(keys[6], 1), 0, NZ - 1).astype(jnp.int32),
    }


TIME_STEP = 0.05
GAMMAS = (8.0 / 15.0, 5.0 / 12.0, 3.0 / 4.0)
ZETAS = (0.0, -17.0 / 60.0, -5.0 / 12.0)
HIGHEST = lax.Precision.HIGHEST


def spectral_table(points):
    row_index = jnp.arange(points, dtype=jnp.int32)[:, None]
    column_index = jnp.arange(points, dtype=jnp.int32)[None, :]
    offset = row_index - column_index
    parity = (1 - 2 * (offset % 2)).astype(jnp.float32)
    phase_angle = (math.pi / points) * offset.astype(jnp.float32)
    cotangent_base = jnp.where(offset == 0, jnp.float32(1.0), jnp.tan(phase_angle))
    return jnp.where(offset == 0, jnp.float32(0.0), 0.5 * parity / cotangent_base)


def derive_streamwise(matrix, velocity):
    return jnp.einsum('jk,cykz->cyjz', matrix, velocity, precision=HIGHEST)


def derive_spanwise(matrix, velocity):
    return jnp.einsum('cyxk,jk->cyxj', velocity, matrix, precision=HIGHEST)


def apply_wall(matrix, velocity):
    return jnp.einsum('jk,ckxz->cjxz', matrix, velocity, precision=HIGHEST)


def explicit_term(baseline, base_dx, base_dy, base_dz, velocity, velocity_dy, stream_table, span_table):
    velocity_dx = derive_streamwise(stream_table, velocity)
    velocity_dz = derive_spanwise(span_table, velocity)
    carried = baseline[0:1] * velocity_dx + baseline[1:2] * velocity_dy + baseline[2:3] * velocity_dz
    sheared = velocity[0:1] * base_dx + velocity[1:2] * base_dy + velocity[2:3] * base_dz
    return -(carried + sheared)


def reference(tangent, base_flow, base_shear, wall_derivative, implicit_inverse, successor, spanwise_shift):
    stream_table = spectral_table(NX)
    span_table = spectral_table(NZ)

    def segment(position):
        initial = lax.dynamic_index_in_dim(tangent, position, 0, keepdims=False)
        baseline = lax.dynamic_index_in_dim(base_flow, position, 0, keepdims=False).astype(jnp.float32)
        base_dy = lax.dynamic_index_in_dim(base_shear, position, 0, keepdims=False).astype(jnp.float32)
        follower = lax.dynamic_index_in_dim(successor, position, 0, keepdims=False).astype(jnp.int32)
        following = lax.dynamic_index_in_dim(tangent, follower, 0, keepdims=False)
        amount = lax.dynamic_index_in_dim(spanwise_shift, position, 0, keepdims=False)
        base_dx = derive_streamwise(stream_table, baseline)
        base_dz = derive_spanwise(span_table, baseline)
        velocity = initial
        velocity_dy = apply_wall(wall_derivative, velocity)
        previous = jnp.zeros_like(velocity)
        for step_number in range(STEPS):
            for section in range(3):
                term = explicit_term(baseline, base_dx, base_dy, base_dz, velocity, velocity_dy, stream_table, span_table)
                right_side = velocity + TIME_STEP * (GAMMAS[section] * term + ZETAS[section] * previous)
                velocity = apply_wall(implicit_inverse[section], right_side)
                previous = term
                if not (step_number == STEPS - 1 and section == 2):
                    velocity_dy = apply_wall(wall_derivative, velocity)
        return jnp.roll(velocity, amount, axis=3) - following

    return lax.map(segment, jnp.arange(SEGS, dtype=jnp.int32))
```

```python
import functools

import numpy as np
import jax
import jax.numpy as jnp
from jax import lax
from jax.experimental import pallas as pl
from jax.experimental.pallas import tpu as pltpu
from jax.sharding import PartitionSpec as P

TIME_STEP = 0.05
GAMMAS = (8.0 / 15.0, 5.0 / 12.0, 3.0 / 4.0)
ZETAS = (0.0, -17.0 / 60.0, -5.0 / 12.0)
SECTIONS = 3
TOP = 32767.0
STEPS_PER_OCTAVE = 64.0
F32 = jnp.float32
BF16 = jnp.bfloat16
VMEM_LIMIT = 60 * 1024 * 1024


def spectral_table(points):
    offset = np.arange(points)[:, None] - np.arange(points)[None, :]
    away = np.where(offset == 0, 1, offset)
    table = 0.5 * (1 - 2 * (offset % 2)) / np.tan(np.pi * away / points)
    return np.where(offset == 0, 0.0, table).astype(np.float32)


def halves(table):
    high = table.astype(jnp.bfloat16)
    low = (table - high.astype(np.float32)).astype(jnp.bfloat16)
    return np.asarray(high), np.asarray(low)


def split(value):
    high = value.astype(BF16)
    return high, (value - high.astype(F32)).astype(BF16)


def dot(left, right):
    return jnp.dot(left, right, preferred_element_type=F32)


class Plan:
    def __init__(self, rows, nx, nz, parts):
        self.rows, self.nx, self.nz, self.parts = rows, nx, nz, parts
        self.cuts = 1 if nx // parts >= 16 else 2
        self.width = nx * self.cuts // parts
        self.depth = nz // self.cuts
        self.lines = rows * parts
        self.scale_rows = -(-rows // 16) * 16

    def rows_of(self, fields):
        return fields * self.rows * self.width

    def piece(self, number):
        along = pl.multiple_of(number // self.cuts * self.width, self.width)
        if self.cuts == 1:
            return pl.ds(along, self.width), pl.ds(0, self.depth)
        across = pl.multiple_of(number % self.cuts * self.depth, self.depth)
        return pl.ds(along, self.width), pl.ds(across, self.depth)


def scale_code(largest):
    return jnp.floor(jnp.log2(jnp.maximum(largest, 1e-35)) * STEPS_PER_OCTAVE) + 2.0


def encode(code):
    return TOP * jnp.exp2(code * (-1.0 / STEPS_PER_OCTAVE))


def decode(code):
    return (1.0 / TOP) * jnp.exp2(code * (1.0 / STEPS_PER_OCTAVE))


def to_short(value):
    return jnp.round(value).astype(jnp.int32).astype(jnp.int16)


def from_short(value):
    return value.astype(jnp.int32).astype(F32)


def column_max(values):
    return functools.reduce(
        jnp.maximum, [jnp.max(jnp.abs(v), axis=0, keepdims=True) for v in values]
    )


def pack_kernel(plan, me_ref, tangent_ref, flow_ref, *rest):
    outs, codes = rest[: plan.parts], rest[plan.parts]
    row = pl.program_id(0)
    me = me_ref[0]
    for d in range(plan.parts):
        along, across = plan.piece(me ^ d)
        values = [tangent_ref[c, 0, along, across] for c in range(3)]
        values.append(flow_ref[0, 0, along, across].astype(F32))
        for first, group in ((0, values[:3]), (3, values[3:])):
            code = scale_code(column_max(group))
            factor = encode(code)
            for k, value in enumerate(group):
                start = pl.multiple_of(((first + k) * plan.rows + row) * plan.width, plan.width)
                outs[d][pl.ds(start, plan.width), :] = to_short(value * factor)
            base = 0 if first == 0 else plan.scale_rows
            codes[d, pl.ds(base + row, 1), :] = code

    @pl.when(row == plan.rows - 1)
    def _():
        for d in range(plan.parts):
            outs[d][plan.rows_of(4) :, :] = codes[d].astype(jnp.int32).astype(jnp.int16)


def pack_start(plan, me, tangent, flow):
    height = plan.rows_of(4) + 2 * plan.scale_rows
    return pl.pallas_call(
        functools.partial(pack_kernel, plan),
        grid_spec=pltpu.PrefetchScalarGridSpec(
            num_scalar_prefetch=1,
            grid=(plan.rows,),
            in_specs=[
                pl.BlockSpec((3, 1, plan.nx, plan.nz), lambda j, *_: (0, j, 0, 0)),
                pl.BlockSpec((1, 1, plan.nx, plan.nz), lambda j, *_: (1, j, 0, 0)),
            ],
            out_specs=[pl.BlockSpec((height, plan.depth), lambda j, *_: (0, 0))] * plan.parts,
            scratch_shapes=[pltpu.VMEM((plan.parts, 2 * plan.scale_rows, plan.depth), F32)],
        ),
        out_shape=[jax.ShapeDtypeStruct((height, plan.depth), jnp.int16)] * plan.parts,
        compiler_params=pltpu.CompilerParams(vmem_limit_bytes=VMEM_LIMIT),
        cost_estimate=pl.CostEstimate(flops=0, transcendentals=0, bytes_accessed=20_000_000),
        name="pack_start",
    )(me, tangent, flow)


def explicit_kernel(plan, received, me_ref, *refs):
    parts = plan.parts
    if received:
        sources, refs = refs[:parts], refs[parts:]
    else:
        tangent_ref, refs = refs[0], refs[1:]
    flow_ref, shear_ref, dx_ref, dz_ref = refs[:4]
    outs = refs[4 : 4 + parts]
    speed, term, codes = refs[4 + parts : 7 + parts]
    row = pl.program_id(0)
    me = me_ref[0]
    nx = plan.nx
    if received:
        scales = refs[7 + parts]

        @pl.when(row == 0)
        def _():
            for d in range(parts):
                scales[d] = decode(from_short(sources[d][plan.rows_of(3) :, :]))

        for d in range(parts):
            along, across = plan.piece(me ^ d)
            for c in range(3):
                start = pl.multiple_of((c * plan.rows + row) * plan.width, plan.width)
                value = from_short(sources[d][pl.ds(start, plan.width), :])
                speed[c, along, across] = value * scales[d, c : c + 1, :]
    else:
        for c in range(3):
            speed[c] = tangent_ref[c, 0]
    for c in range(3):
        high, low = split(speed[c])
        flow = flow_ref[c, 0]
        both = dot(dx_ref[...], high)
        along_x = both[:nx] + both[nx:] + dot(dx_ref[:nx, :], low)
        along_z = dot(high, dz_ref[0]) + (dot(low, dz_ref[0]) + dot(high, dz_ref[1]))
        carried = flow_ref[0, 0].astype(F32) * along_x + flow_ref[2, 0].astype(F32) * along_z
        both = dot(dx_ref[...], flow)
        base_dx = both[:nx] + both[nx:]
        base_dz = dot(flow, dz_ref[0]) + dot(flow, dz_ref[1])
        sheared = (
            speed[0] * base_dx + speed[1] * shear_ref[c, 0].astype(F32) + speed[2] * base_dz
        )
        term[c] = -(carried + sheared)
    for d in range(parts):
        along, across = plan.piece(me ^ d)
        values = [term[c, along, across] for c in range(3)]
        code = scale_code(column_max(values))
        factor = encode(code)
        for c in range(3):
            start = pl.multiple_of((c * plan.rows + row) * plan.width, plan.width)
            outs[d][pl.ds(start, plan.width), :] = to_short(values[c] * factor)
        codes[d, pl.ds(row, 1), :] = code

    @pl.when(row == plan.rows - 1)
    def _():
        for d in range(parts):
            outs[d][plan.rows_of(3) :, :] = codes[d].astype(jnp.int32).astype(jnp.int16)


def explicit(plan, me, velocity, flow, shear, dx, dz):
    received = isinstance(velocity, list)
    parts = plan.parts
    height = plan.rows_of(3) + plan.scale_rows
    field = pl.BlockSpec((3, 1, plan.nx, plan.nz), lambda j, *_: (0, j, 0, 0))
    scratch = [
        pltpu.VMEM((3, plan.nx, plan.nz), F32),
        pltpu.VMEM((3, plan.nx, plan.nz), F32),
        pltpu.VMEM((parts, plan.scale_rows, plan.depth), F32),
    ]
    if received:
        first = [
            pl.BlockSpec(v.shape, lambda j, *_: (0, 0), pipeline_mode=pl.Buffered(1))
            for v in velocity
        ]
        scratch.append(pltpu.VMEM((parts, 16, plan.depth), F32))
    else:
        first, velocity = [field], [velocity]
    return pl.pallas_call(
        functools.partial(explicit_kernel, plan, received),
        grid_spec=pltpu.PrefetchScalarGridSpec(
            num_scalar_prefetch=1,
            grid=(plan.rows,),
            in_specs=first
            + [
                field,
                field,
                pl.BlockSpec(dx.shape, lambda j, *_: (0, 0)),
                pl.BlockSpec(dz.shape, lambda j, *_: (0, 0, 0)),
            ],
            out_specs=[pl.BlockSpec((height, plan.depth), lambda j, *_: (0, 0))] * parts,
            scratch_shapes=scratch,
        ),
        out_shape=[jax.ShapeDtypeStruct((height, plan.depth), jnp.int16)] * parts,
        compiler_params=pltpu.CompilerParams(vmem_limit_bytes=VMEM_LIMIT),
        cost_estimate=pl.CostEstimate(
            flops=12_000_000_000, transcendentals=0, bytes_accessed=40_000_000
        ),
        name="explicit",
    )(me, *velocity, flow, shear, dx, dz)


def stacked(matrices):
    rows = []
    for matrix in matrices:
        high, low = split(matrix)
        rows.append(jnp.concatenate([high, high], axis=1))
        rows.append(jnp.concatenate([low, jnp.zeros_like(low)], axis=1))
    return jnp.concatenate(rows, axis=0)


def precise_dot(left, right):
    high, low = split(left)
    right_high, right_low = split(right)
    return dot(high, right_high) + (dot(low, right_high) + dot(high, right_low))


def put(field, rows, value):
    for half in range(field.shape[0]):
        field[half, rows, :] = value[:, half * 128 : half * 128 + 128]


def get(field, rows):
    return jnp.concatenate([field[half, rows, :] for half in range(field.shape[0])], axis=1)


def unpack_lines(plan, me, sources, scales, field):
    for d, (source, scale) in enumerate(zip(sources, scales)):
        scale = decode(from_short(scale[...]))
        first = pl.multiple_of((me ^ d) * plan.rows_of(1), plan.width)
        for j in range(plan.rows):
            value = from_short(source[j * plan.width : (j + 1) * plan.width, :])
            put(field, pl.ds(first + j * plan.width, plan.width), value * scale[j : j + 1, :])


def first_lines_kernel(plan, me_ref, *refs):
    parts, lines = plan.parts, plan.lines
    values, scales = refs[:parts], refs[parts : 2 * parts]
    flows, flow_scales = refs[2 * parts : 3 * parts], refs[3 * parts : 4 * parts]
    wall_ref, right_ref, turned_ref, flow_ref, field, table = refs[4 * parts :]
    me = me_ref[0]

    @pl.when(pl.program_id(0) == 0)
    def _():
        table[...] = stacked([wall_ref[...]])
        unpack_lines(plan, me, flows, flow_scales, field)

        def turn(r, carry):
            flow_ref[r] = get(field, pl.ds(r, lines, stride=plan.width))
            return carry

        lax.fori_loop(0, plan.width, turn, 0)

    unpack_lines(plan, me, values, scales, field)

    def line(r, carry):
        value = get(field, pl.ds(r, lines, stride=plan.width))
        product = dot(table[...], jnp.concatenate(split(value), axis=0))
        turned = -(flow_ref[r] * (product[:lines] + product[lines:]))
        turned_ref[0, r] = turned
        right_ref[0, r] = value + (TIME_STEP * GAMMAS[0]) * turned
        return carry

    lax.fori_loop(0, plan.width, line, 0)


def first_lines(plan, me, blocks, wall):
    parts, lines, width, depth = plan.parts, plan.lines, plan.width, plan.depth
    at = plan.rows_of(4) // plan.scale_rows
    part = (plan.rows_of(1), depth)
    codes = (plan.scale_rows, depth)
    state = jax.ShapeDtypeStruct((3, width, lines, depth), F32)
    state_spec = pl.BlockSpec((1, width, lines, depth), lambda c, *_: (c, 0, 0, 0))
    return pl.pallas_call(
        functools.partial(first_lines_kernel, plan),
        grid_spec=pltpu.PrefetchScalarGridSpec(
            num_scalar_prefetch=1,
            grid=(3,),
            in_specs=[pl.BlockSpec(part, lambda c, *_: (c, 0))] * parts
            + [pl.BlockSpec(codes, lambda c, *_: (at, 0))] * parts
            + [pl.BlockSpec(part, lambda c, *_: (3, 0))] * parts
            + [pl.BlockSpec(codes, lambda c, *_: (at + 1, 0))] * parts
            + [pl.BlockSpec(wall.shape, lambda c, *_: (0, 0))],
            out_specs=[
                state_spec,
                state_spec,
                pl.BlockSpec((width, lines, depth), lambda c, *_: (0, 0, 0)),
            ],
            scratch_shapes=[
                pltpu.VMEM((depth // 128, lines * width, 128), F32),
                pltpu.VMEM((2 * lines, 2 * lines), BF16),
            ],
        ),
        out_shape=[state, state, jax.ShapeDtypeStruct((width, lines, depth), F32)],
        compiler_params=pltpu.CompilerParams(vmem_limit_bytes=VMEM_LIMIT),
        cost_estimate=pl.CostEstimate(
            flops=1_000_000_000, transcendentals=0, bytes_accessed=30_000_000
        ),
        name="first_lines",
    )(me, *(blocks * 4), wall)


def lines_kernel(plan, section, me_ref, *refs):
    parts, lines = plan.parts, plan.lines
    last = section == SECTIONS - 1
    values, scales, refs = refs[:parts], refs[parts : 2 * parts], refs[2 * parts :]
    if last:
        wall_ref, solve_ref, right_ref = refs[:3]
        outs, (field, table, codes) = refs[3 : 3 + parts], refs[3 + parts :]
    else:
        wall_ref, solve_ref, right_ref, turned_ref, flow_ref = refs[:5]
        outs, refs = refs[5 : 5 + parts], refs[5 + parts :]
        right_out, turned_out, field, table, codes = refs
    me = me_ref[0]
    component = pl.program_id(0)

    @pl.when(component == 0)
    def _():
        solve = solve_ref[0]
        tables = [solve] if last else [solve, precise_dot(wall_ref[...], solve)]
        table[...] = stacked(tables)
        codes[...] = jnp.zeros_like(codes)

    unpack_lines(plan, me, values, scales, field)

    def line(r, carry):
        here = pl.ds(r, lines, stride=plan.width)
        term = get(field, here)
        right = right_ref[0, r] + (TIME_STEP * GAMMAS[section]) * term
        product = dot(table[...], jnp.concatenate(split(right), axis=0))
        value = product[:lines] + product[lines : 2 * lines]
        put(field, here, value)
        if not last:
            slope = product[2 * lines : 3 * lines] + product[3 * lines :]
            turned = -(flow_ref[r] * slope)
            past = term + turned_ref[0, r]
            turned_out[0, r] = turned
            right_out[0, r] = (
                value
                + (TIME_STEP * ZETAS[section + 1]) * past
                + (TIME_STEP * GAMMAS[section + 1]) * turned
            )
        return carry

    lax.fori_loop(0, plan.width, line, 0)

    for d in range(parts):
        first = pl.multiple_of((me ^ d) * plan.rows_of(1), plan.width)
        chunk = [
            get(field, pl.ds(first + j * plan.width, plan.width)) for j in range(plan.rows)
        ]
        code = scale_code(column_max(chunk))
        factor = encode(code)
        for j in range(plan.rows):
            start = pl.multiple_of((component * plan.rows + j) * plan.width, plan.width)
            outs[d][pl.ds(start, plan.width), :] = to_short(chunk[j] * factor)
        codes[d, pl.ds(component, 1), :] = code

    @pl.when(component == 2)
    def _():
        for d in range(parts):
            outs[d][plan.rows_of(3) :, :] = codes[d].astype(jnp.int32).astype(jnp.int16)


def advance_lines(plan, section, me, blocks, wall, solves, right, turned, flow):
    parts, lines, width, depth = plan.parts, plan.lines, plan.width, plan.depth
    last = section == SECTIONS - 1
    at = plan.rows_of(3) // plan.scale_rows
    height = plan.rows_of(3) + 16
    state_spec = pl.BlockSpec((1, width, lines, depth), lambda c, *_: (c, 0, 0, 0))
    in_specs = (
        [pl.BlockSpec((plan.rows_of(1), depth), lambda c, *_: (c, 0))] * parts
        + [pl.BlockSpec((plan.scale_rows, depth), lambda c, *_: (at, 0))] * parts
        + [
            pl.BlockSpec(wall.shape, lambda c, *_: (0, 0)),
            pl.BlockSpec((1, lines, lines), lambda c, *_: (section, 0, 0)),
            state_spec,
        ]
    )
    args = [me, *blocks, *blocks, wall, solves, right]
    out_specs = [pl.BlockSpec((height, depth), lambda c, *_: (0, 0))] * parts
    out_shape = [jax.ShapeDtypeStruct((height, depth), jnp.int16)] * parts
    copies = 2
    if not last:
        in_specs += [
            state_spec,
            pl.BlockSpec(flow.shape, lambda c, *_: (0, 0, 0), pipeline_mode=pl.Buffered(1)),
        ]
        args += [turned, flow]
        out_specs = out_specs + [state_spec, state_spec]
        out_shape = out_shape + [jax.ShapeDtypeStruct(right.shape, F32)] * 2
        copies = 4
    results = pl.pallas_call(
        functools.partial(lines_kernel, plan, section),
        grid_spec=pltpu.PrefetchScalarGridSpec(
            num_scalar_prefetch=1,
            grid=(3,),
            in_specs=in_specs,
            out_specs=out_specs,
            scratch_shapes=[
                pltpu.VMEM((depth // 128, lines * width, 128), F32),
                pltpu.VMEM((copies * lines, 2 * lines), BF16),
                pltpu.VMEM((parts, 16, depth), F32),
            ],
        ),
        out_shape=out_shape,
        compiler_params=pltpu.CompilerParams(vmem_limit_bytes=VMEM_LIMIT),
        cost_estimate=pl.CostEstimate(
            flops=2_000_000_000, transcendentals=0, bytes_accessed=50_000_000
        ),
        name="advance_lines",
    )(*args)
    return results[:parts], results[parts:]


def result_kernel(plan, me_ref, shift_ref, pick_ref, *refs):
    parts = plan.parts
    sources = refs[:parts]
    near_ref, far_ref, out_ref, speed, scales = refs[parts:]
    row = pl.program_id(0)
    me = me_ref[0]

    @pl.when(row == 0)
    def _():
        for d in range(parts):
            scales[d] = decode(from_short(sources[d][plan.rows_of(3) :, :]))

    for d in range(parts):
        along, across = plan.piece(me ^ d)
        for c in range(3):
            start = pl.multiple_of((c * plan.rows + row) * plan.width, plan.width)
            value = from_short(sources[d][pl.ds(start, plan.width), :])
            speed[c, along, across] = value * scales[d, c : c + 1, :]
    far = pick_ref[0] != 0
    for c in range(3):
        rolled = pltpu.roll(speed[c], shift_ref[0], axis=1)

        @pl.when(far)
        def _():
            out_ref[c, 0] = rolled - far_ref[c, 0]

        @pl.when(jnp.logical_not(far))
        def _():
            out_ref[c, 0] = rolled - near_ref[c, 0]


def result(plan, me, shift, pick, blocks, near, far):
    parts = plan.parts
    block = (3, 1, plan.nx, plan.nz)
    return pl.pallas_call(
        functools.partial(result_kernel, plan),
        grid_spec=pltpu.PrefetchScalarGridSpec(
            num_scalar_prefetch=3,
            grid=(plan.rows,),
            in_specs=[
                pl.BlockSpec(b.shape, lambda j, *_: (0, 0), pipeline_mode=pl.Buffered(1))
                for b in blocks
            ]
            + [
                pl.BlockSpec(block, lambda j, me, shift, pick: (0, j * (1 - pick[0]), 0, 0)),
                pl.BlockSpec(block, lambda j, me, shift, pick: (0, j * pick[0], 0, 0)),
            ],
            out_specs=pl.BlockSpec(block, lambda j, *_: (0, j, 0, 0)),
            scratch_shapes=[
                pltpu.VMEM((3, plan.nx, plan.nz), F32),
                pltpu.VMEM((parts, 16, plan.depth), F32),
            ],
        ),
        out_shape=jax.ShapeDtypeStruct((3, plan.rows, plan.nx, plan.nz), F32),
        compiler_params=pltpu.CompilerParams(vmem_limit_bytes=VMEM_LIMIT),
        cost_estimate=pl.CostEstimate(flops=0, transcendentals=0, bytes_accessed=25_000_000),
        name="result",
    )(me, shift, pick, *blocks, near, far)


def exchange(blocks):
    parts = len(blocks)
    moved = [blocks[0]]
    for d in range(1, parts):
        moved.append(lax.ppermute(blocks[d], "grid", [(i, i ^ d) for i in range(parts)]))
    return moved


def behind(block, distance):
    devices = lax.axis_size("seg")
    route = [((i + distance) % devices, i) for i in range(devices)]
    return lax.ppermute(block, "seg", route)


def successors(tangent, successor):
    segments = lax.axis_size("seg")
    position = lax.axis_index("seg")
    labels = jnp.arange(successor.shape[0], dtype=jnp.int32)
    ahead = jnp.sum(jnp.where(labels == position, successor, 0))
    offset = (ahead - position) % segments
    near = behind(tangent, 1)
    bits = (segments - 1).bit_length()
    for bit in range(1, bits - 1):
        near = jnp.where(offset // (1 << bit) % 2 == 1, behind(near, 1 << bit), near)
    far = behind(near, 1 << (bits - 1))
    return near, far, (offset // (1 << (bits - 1)) % 2).reshape(1)


def shards(
    tangent, base_flow, base_shear, wall_derivative, implicit_inverse, successor, spanwise_shift
):
    tangent, flow, shear = tangent[0], base_flow[0], base_shear[0]
    _, rows, nx, nz = tangent.shape
    plan = Plan(rows, nx, nz, lax.axis_size("grid"))
    me = lax.axis_index("grid").astype(jnp.int32).reshape(1)
    dx = jnp.asarray(np.concatenate(halves(spectral_table(nx)), axis=0))
    dz = jnp.asarray(np.stack(halves(spectral_table(nz).T)))

    start = exchange(pack_start(plan, me, tangent, flow))
    term = exchange(explicit(plan, me, tangent, flow, shear, dx, dz))
    near, far, pick = successors(tangent, successor)
    right, turned, wall_flow = first_lines(plan, me, start, wall_derivative)
    for section in range(SECTIONS):
        value, state = advance_lines(
            plan, section, me, term, wall_derivative, implicit_inverse, right, turned, wall_flow
        )
        value = exchange(value)
        if section < SECTIONS - 1:
            right, turned = state
            term = exchange(explicit(plan, me, value, flow, shear, dx, dz))
    return result(plan, me, spanwise_shift, pick, value, near, far)[None]


def solution(mesh):
    placed = P("seg", None, "grid", None, None)
    return jax.shard_map(
        shards,
        mesh=mesh,
        in_specs=(placed, placed, placed, P(), P(), P(), P("seg")),
        out_specs=placed,
        check_vma=False,
    )
```

```python
import functools

import numpy as np
import jax
import jax.numpy as jnp
from jax import lax
from jax.experimental import pallas as pl
from jax.experimental.pallas import tpu as pltpu
from jax.sharding import PartitionSpec as P

TIME_STEP = 0.05
GAMMAS = (8.0 / 15.0, 5.0 / 12.0, 3.0 / 4.0)
ZETAS = (0.0, -17.0 / 60.0, -5.0 / 12.0)
SECTIONS = 3
WHOLE = (True, False)
GROUPS = ((0,), (1, 2))
TOP = 32767.0
STEPS_PER_OCTAVE = 64.0
F32 = jnp.float32
BF16 = jnp.bfloat16
VMEM_LIMIT = 60 * 1024 * 1024


def spectral_table(points):
    offset = np.arange(points)[:, None] - np.arange(points)[None, :]
    away = np.where(offset == 0, 1, offset)
    table = 0.5 * (1 - 2 * (offset % 2)) / np.tan(np.pi * away / points)
    return np.where(offset == 0, 0.0, table).astype(np.float32)


def halves(table):
    high = table.astype(jnp.bfloat16)
    low = (table - high.astype(np.float32)).astype(jnp.bfloat16)
    return np.asarray(high), np.asarray(low)


def split(value):
    high = value.astype(BF16)
    return high, (value - high.astype(F32)).astype(BF16)


def dot(left, right):
    return jnp.dot(left, right, preferred_element_type=F32)


def aligned(value, multiple):
    return value if isinstance(value, int) else pl.multiple_of(value, multiple)


def partner(whole, me, d):
    return d if whole else me ^ d


class Plan:
    def __init__(self, rows, nx, nz, parts):
        self.rows, self.nx, self.nz, self.parts = rows, nx, nz, parts
        self.cuts = 1 if nx // parts >= 16 else 2
        self.width = nx * self.cuts // parts
        self.depth = nz // self.cuts
        self.lines = rows * parts
        self.scale_rows = -(-rows // 16) * 16
        early = max(rows // 3, 1)
        self.spans = ((0, early), (early, rows - early))

    def rows_of(self, fields, rows=None):
        return fields * (rows or self.rows) * self.width

    def piece(self, number):
        along = aligned(number // self.cuts * self.width, self.width)
        if self.cuts == 1:
            return pl.ds(along, self.width), pl.ds(0, self.depth)
        across = aligned(number % self.cuts * self.depth, self.depth)
        return pl.ds(along, self.width), pl.ds(across, self.depth)


def scale_code(largest):
    return jnp.floor(jnp.log2(jnp.maximum(largest, 1e-35)) * STEPS_PER_OCTAVE) + 2.0


def encode(code):
    return TOP * jnp.exp2(code * (-1.0 / STEPS_PER_OCTAVE))


def decode(code):
    return (1.0 / TOP) * jnp.exp2(code * (1.0 / STEPS_PER_OCTAVE))


def to_short(value):
    return jnp.round(value).astype(jnp.int32).astype(jnp.int16)


def from_short(value):
    return value.astype(jnp.int32).astype(F32)


def column_max(values):
    return functools.reduce(
        jnp.maximum, [jnp.max(jnp.abs(v), axis=0, keepdims=True) for v in values]
    )


def pack_kernel(plan, tangent_ref, flow_ref, out_ref, codes):
    row = pl.program_id(0)
    for d in range(plan.parts):
        along, across = plan.piece(d)
        values = [tangent_ref[c, 0, along, across] for c in range(3)]
        values.append(flow_ref[0, 0, along, across].astype(F32))
        for first, group in ((0, values[:3]), (3, values[3:])):
            code = scale_code(column_max(group))
            factor = encode(code)
            for k, value in enumerate(group):
                start = pl.multiple_of(((first + k) * plan.rows + row) * plan.width, plan.width)
                out_ref[d, pl.ds(start, plan.width), :] = to_short(value * factor)
            base = 0 if first == 0 else plan.scale_rows
            codes[d, pl.ds(base + row, 1), :] = code

    @pl.when(row == plan.rows - 1)
    def _():
        for d in range(plan.parts):
            out_ref[d, plan.rows_of(4) :, :] = codes[d].astype(jnp.int32).astype(jnp.int16)


def pack_start(plan, tangent, flow):
    shape = (plan.parts, plan.rows_of(4) + 2 * plan.scale_rows, plan.depth)
    return pl.pallas_call(
        functools.partial(pack_kernel, plan),
        grid=(plan.rows,),
        in_specs=[
            pl.BlockSpec((3, 1, plan.nx, plan.nz), lambda j: (0, j, 0, 0)),
            pl.BlockSpec((1, 1, plan.nx, plan.nz), lambda j: (1, j, 0, 0)),
        ],
        out_specs=pl.BlockSpec(shape, lambda j: (0, 0, 0)),
        scratch_shapes=[pltpu.VMEM((plan.parts, 2 * plan.scale_rows, plan.depth), F32)],
        out_shape=jax.ShapeDtypeStruct(shape, jnp.int16),
        compiler_params=pltpu.CompilerParams(vmem_limit_bytes=VMEM_LIMIT),
        cost_estimate=pl.CostEstimate(flops=0, transcendentals=0, bytes_accessed=20_000_000),
        name="pack_start",
    )(tangent, flow)


def pieces(plan, whole):
    return 1 if whole else plan.parts


def each(plan, whole, refs):
    return [refs[0].at[d] for d in range(plan.parts)] if whole else list(refs)


def block_specs(plan, whole, rows, depth, index, **more):
    if whole:
        return [pl.BlockSpec((plan.parts, rows, depth), lambda i, *_: (0, index(i), 0), **more)]
    return [pl.BlockSpec((rows, depth), lambda i, *_: (index(i), 0), **more)] * plan.parts


def block_shapes(plan, whole, rows):
    shape = (plan.parts, rows, plan.depth) if whole else (rows, plan.depth)
    return [jax.ShapeDtypeStruct(shape, jnp.int16)] * pieces(plan, whole)


def flat(groups):
    return [block for blocks in groups for block in blocks]


def grouped(plan, refs):
    lists = []
    for whole in WHOLE:
        count = pieces(plan, whole)
        lists.append(refs[:count])
        refs = refs[count:]
    return lists, refs


def receive(plan, me, row, sources, scales, speed):
    for whole, group, blocks, factors in zip(WHOLE, GROUPS, sources, scales):
        for d in range(plan.parts):
            along, across = plan.piece(partner(whole, me, d))
            for k, c in enumerate(group):
                start = pl.multiple_of((k * plan.rows + row) * plan.width, plan.width)
                value = from_short(blocks[d][pl.ds(start, plan.width), :])
                speed[c, along, across] = value * factors[d, k : k + 1, :]


def prepare(plan, sources, scales):
    for group, blocks, factors in zip(GROUPS, sources, scales):
        for d in range(plan.parts):
            factors[d] = decode(from_short(blocks[d][plan.rows_of(len(group)) :, :]))


def blockwise(plan, refs):
    lists, rest = grouped(plan, refs)
    return [each(plan, whole, blocks) for whole, blocks in zip(WHOLE, lists)], rest


def explicit_kernel(plan, which, received, me_ref, *refs):
    parts, nx = plan.parts, plan.nx
    if received:
        sources, refs = blockwise(plan, refs)
    else:
        tangent_ref, refs = refs[0], refs[1:]
    flow_ref, shear_ref, dx_ref, dz_ref = refs[:4]
    refs = refs[4:]
    if received:
        base_dx_ref, base_dz_ref, refs = refs[0], refs[1], refs[2:]
    whole, (above, rows) = WHOLE[which], plan.spans[which]
    count = pieces(plan, whole)
    outs, refs = each(plan, whole, refs[:count]), refs[count:]
    if not received:
        base_dx_ref, base_dz_ref, refs = refs[0], refs[1], refs[2:]
    speed, term, codes = refs[:3]
    scales = refs[3:]
    row = pl.program_id(0)
    me = me_ref[0]
    if received:

        @pl.when(row == 0)
        def _():
            prepare(plan, sources, scales)

        receive(plan, me, above + row, sources, scales, speed)
    else:
        for c in range(3):
            speed[c] = tangent_ref[c, 0]
    for c in range(3):
        if not received:
            flow = flow_ref[c, 0]
            both = dot(dx_ref[...], flow)
            base_dx_ref[c, 0] = both[:nx] + both[nx:]
            base_dz_ref[c, 0] = dot(flow, dz_ref[0]) + dot(flow, dz_ref[1])
        high, low = split(speed[c])
        both = dot(dx_ref[...], high)
        along_x = both[:nx] + both[nx:] + dot(dx_ref[:nx, :], low)
        along_z = dot(high, dz_ref[0]) + (dot(low, dz_ref[0]) + dot(high, dz_ref[1]))
        carried = flow_ref[0, 0].astype(F32) * along_x + flow_ref[2, 0].astype(F32) * along_z
        sheared = (
            speed[0] * base_dx_ref[c, 0]
            + speed[1] * shear_ref[c, 0].astype(F32)
            + speed[2] * base_dz_ref[c, 0]
        )
        term[c] = -(carried + sheared)
    for d in range(parts):
        along, across = plan.piece(partner(whole, me, d))
        values = [term[c, along, across] for c in range(3)]
        code = scale_code(column_max(values))
        factor = encode(code)
        for c, value in enumerate(values):
            start = pl.multiple_of((c * rows + row) * plan.width, plan.width)
            outs[d][pl.ds(start, plan.width), :] = to_short(value * factor)
        codes[d, pl.ds(row, 1), :] = code

    @pl.when(row == rows - 1)
    def _():
        for d in range(parts):
            outs[d][plan.rows_of(3, rows) :, :] = codes[d].astype(jnp.int32).astype(jnp.int16)


def whole_blocks(plan):
    specs = []
    for whole, group in zip(WHOLE, GROUPS):
        height = plan.rows_of(len(group)) + 16
        once = dict(pipeline_mode=pl.Buffered(1))
        specs += block_specs(plan, whole, height, plan.depth, lambda j: 0, **once)
    return specs


def explicit(plan, which, me, velocity, flow, shear, dx, dz, bases=None):
    received = bases is not None
    parts = plan.parts
    whole, (above, rows) = WHOLE[which], plan.spans[which]
    height = plan.rows_of(3, rows) + plan.scale_rows
    block = (3, 1, plan.nx, plan.nz)
    field = pl.BlockSpec(block, lambda j, *_: (0, above + j, 0, 0))
    own = pl.BlockSpec(block, lambda j, *_: (0, j, 0, 0))
    scratch = [
        pltpu.VMEM((3, plan.nx, plan.nz), F32),
        pltpu.VMEM((3, plan.nx, plan.nz), F32),
        pltpu.VMEM((parts, plan.scale_rows, plan.depth), F32),
    ]
    out_specs = block_specs(plan, whole, height, plan.depth, lambda j: 0)
    out_shape = block_shapes(plan, whole, height)
    if received:
        first, more = whole_blocks(plan), [own, own]
        velocity = flat(velocity)
        scratch += [pltpu.VMEM((parts, 16, plan.depth), F32)] * len(GROUPS)
    else:
        first, velocity, bases, more = [field], [velocity], [], []
        out_specs += [own, own]
        out_shape += [jax.ShapeDtypeStruct((3, rows, plan.nx, plan.nz), F32)] * 2
    results = pl.pallas_call(
        functools.partial(explicit_kernel, plan, which, received),
        grid_spec=pltpu.PrefetchScalarGridSpec(
            num_scalar_prefetch=1,
            grid=(rows,),
            in_specs=first
            + [
                field,
                field,
                pl.BlockSpec(dx.shape, lambda j, *_: (0, 0)),
                pl.BlockSpec(dz.shape, lambda j, *_: (0, 0, 0)),
            ]
            + more,
            out_specs=out_specs,
            scratch_shapes=scratch,
        ),
        out_shape=out_shape,
        compiler_params=pltpu.CompilerParams(vmem_limit_bytes=VMEM_LIMIT),
        cost_estimate=pl.CostEstimate(
            flops=1_000_000_000 * rows, transcendentals=0, bytes_accessed=4_000_000 * rows
        ),
        name="explicit",
    )(me, *velocity, flow, shear, dx, dz, *bases)
    count = pieces(plan, whole)
    return exchange(plan, whole, results[:count]), results[count:]


def stacked(matrices):
    rows = []
    for matrix in matrices:
        high, low = split(matrix)
        rows.append(jnp.concatenate([high, high], axis=1))
        rows.append(jnp.concatenate([low, jnp.zeros_like(low)], axis=1))
    return jnp.concatenate(rows, axis=0)


def precise_dot(left, right):
    high, low = split(left)
    right_high, right_low = split(right)
    return dot(high, right_high) + (dot(low, right_high) + dot(high, right_low))


def put(field, rows, value):
    for half in range(field.shape[0]):
        field[half, rows, :] = value[:, half * 128 : half * 128 + 128]


def get(field, rows):
    return jnp.concatenate([field[half, rows, :] for half in range(field.shape[0])], axis=1)


def unpack_lines(plan, whole, me, span, sources, scales, field):
    above, rows = span
    for d, (source, scale) in enumerate(zip(sources, scales)):
        scale = decode(from_short(scale[...]))
        first = aligned(partner(whole, me, d) * plan.rows_of(1), plan.width)
        for j in range(rows):
            value = from_short(source[j * plan.width : (j + 1) * plan.width, :])
            here = pl.ds(first + (above + j) * plan.width, plan.width)
            put(field, here, value * scale[j : j + 1, :])


def first_lines_kernel(plan, *refs):
    lines = plan.lines
    values, scales, flows, flow_scales = (each(plan, True, refs[i : i + 1]) for i in range(4))
    wall_ref, right_ref, turned_ref, flow_ref, field, table = refs[4:]

    @pl.when(pl.program_id(0) == 0)
    def _():
        table[...] = stacked([wall_ref[...]])
        unpack_lines(plan, True, None, (0, plan.rows), flows, flow_scales, field)

        def turn(r, carry):
            flow_ref[r] = get(field, pl.ds(r, lines, stride=plan.width))
            return carry

        lax.fori_loop(0, plan.width, turn, 0)

    unpack_lines(plan, True, None, (0, plan.rows), values, scales, field)

    def line(r, carry):
        value = get(field, pl.ds(r, lines, stride=plan.width))
        product = dot(table[...], jnp.concatenate(split(value), axis=0))
        turned = -(flow_ref[r] * (product[:lines] + product[lines:]))
        turned_ref[0, r] = turned
        right_ref[0, r] = value + (TIME_STEP * GAMMAS[0]) * turned
        return carry

    lax.fori_loop(0, plan.width, line, 0, unroll=4)


def first_lines(plan, blocks, wall):
    lines, width, depth = plan.lines, plan.width, plan.depth
    at = plan.rows_of(4) // plan.scale_rows
    rows, codes = plan.rows_of(1), plan.scale_rows
    state = jax.ShapeDtypeStruct((3, width, lines, depth), F32)
    state_spec = pl.BlockSpec((1, width, lines, depth), lambda c: (c, 0, 0, 0))
    return pl.pallas_call(
        functools.partial(first_lines_kernel, plan),
        grid=(3,),
        in_specs=block_specs(plan, True, rows, depth, lambda c: c)
        + block_specs(plan, True, codes, depth, lambda c: at)
        + block_specs(plan, True, rows, depth, lambda c: 3)
        + block_specs(plan, True, codes, depth, lambda c: at + 1)
        + [pl.BlockSpec(wall.shape, lambda c: (0, 0))],
        out_specs=[
            state_spec,
            state_spec,
            pl.BlockSpec((width, lines, depth), lambda c: (0, 0, 0)),
        ],
        scratch_shapes=[
            pltpu.VMEM((depth // 128, lines * width, 128), F32),
            pltpu.VMEM((2 * lines, 2 * lines), BF16),
        ],
        out_shape=[state, state, jax.ShapeDtypeStruct((width, lines, depth), F32)],
        compiler_params=pltpu.CompilerParams(vmem_limit_bytes=VMEM_LIMIT),
        cost_estimate=pl.CostEstimate(
            flops=1_000_000_000, transcendentals=0, bytes_accessed=30_000_000
        ),
        name="first_lines",
    )(blocks, blocks, blocks, blocks, wall)


def lines_kernel(plan, section, group, whole, me_ref, *refs):
    parts, lines = plan.parts, plan.lines
    last = section == SECTIONS - 1
    count = pieces(plan, whole)
    values, refs = blockwise(plan, refs)
    scales, refs = blockwise(plan, refs)
    if last:
        wall_ref, solve_ref, right_ref = refs[:3]
        outs, (field, table, codes) = refs[3 : 3 + count], refs[3 + count :]
    else:
        wall_ref, solve_ref, right_ref, turned_ref, flow_ref = refs[:5]
        outs, refs = refs[5 : 5 + count], refs[5 + count :]
        right_out, turned_out, field, table, codes = refs
    outs = each(plan, whole, outs)
    me = me_ref[0]
    component = pl.program_id(0)

    @pl.when(component == 0)
    def _():
        solve = solve_ref[0]
        tables = [solve] if last else [solve, precise_dot(wall_ref[...], solve)]
        table[...] = stacked(tables)
        codes[...] = jnp.zeros_like(codes)

    for g in range(len(WHOLE)):
        unpack_lines(plan, WHOLE[g], me, plan.spans[g], values[g], scales[g], field)

    def line(r, carry):
        here = pl.ds(r, lines, stride=plan.width)
        term = get(field, here)
        right = right_ref[0, r] + (TIME_STEP * GAMMAS[section]) * term
        product = dot(table[...], jnp.concatenate(split(right), axis=0))
        value = product[:lines] + product[lines : 2 * lines]
        put(field, here, value)
        if not last:
            slope = product[2 * lines : 3 * lines] + product[3 * lines :]
            turned = -(flow_ref[r] * slope)
            past = term + turned_ref[0, r]
            turned_out[0, r] = turned
            right_out[0, r] = (
                value
                + (TIME_STEP * ZETAS[section + 1]) * past
                + (TIME_STEP * GAMMAS[section + 1]) * turned
            )
        return carry

    lax.fori_loop(0, plan.width, line, 0, unroll=4)

    for d in range(parts):
        first = aligned(partner(whole, me, d) * plan.rows_of(1), plan.width)
        chunk = [
            get(field, pl.ds(first + j * plan.width, plan.width)) for j in range(plan.rows)
        ]
        code = scale_code(column_max(chunk))
        factor = encode(code)
        for j in range(plan.rows):
            start = pl.multiple_of((component * plan.rows + j) * plan.width, plan.width)
            outs[d][pl.ds(start, plan.width), :] = to_short(chunk[j] * factor)
        codes[d, pl.ds(component, 1), :] = code

    @pl.when(component == len(group) - 1)
    def _():
        for d in range(parts):
            outs[d][plan.rows_of(len(group)) :, :] = codes[d].astype(jnp.int32).astype(jnp.int16)


def advance_lines(plan, section, group, whole, me, blocks, wall, solves, right, turned, flow):
    lines, width, depth = plan.lines, plan.width, plan.depth
    last = section == SECTIONS - 1
    height = plan.rows_of(len(group)) + 16
    skip = group[0] if right.shape[0] == 3 else 0
    value_specs, scale_specs = [], []
    for kind, (_, rows) in zip(WHOLE, plan.spans):
        at = plan.rows_of(3, rows) // plan.scale_rows
        value_specs += block_specs(plan, kind, plan.rows_of(1, rows), depth, lambda c: c + group[0])
        scale_specs += block_specs(plan, kind, plan.scale_rows, depth, lambda c, at=at: at)
    state_spec = pl.BlockSpec((1, width, lines, depth), lambda c, *_: (c, 0, 0, 0))
    read_spec = pl.BlockSpec((1, width, lines, depth), lambda c, *_: (c + skip, 0, 0, 0))
    in_specs = (
        value_specs
        + scale_specs
        + [
            pl.BlockSpec(wall.shape, lambda c, *_: (0, 0)),
            pl.BlockSpec((1, lines, lines), lambda c, *_: (section, 0, 0)),
            read_spec,
        ]
    )
    args = [me, *flat(blocks), *flat(blocks), wall, solves, right]
    out_specs = block_specs(plan, whole, height, depth, lambda c: 0)
    out_shape = block_shapes(plan, whole, height)
    copies = 2
    if not last:
        in_specs += [
            read_spec,
            pl.BlockSpec(flow.shape, lambda c, *_: (0, 0, 0), pipeline_mode=pl.Buffered(1)),
        ]
        args += [turned, flow]
        out_specs = out_specs + [state_spec, state_spec]
        state = jax.ShapeDtypeStruct((len(group), width, lines, depth), F32)
        out_shape = out_shape + [state, state]
        copies = 4
    results = pl.pallas_call(
        functools.partial(lines_kernel, plan, section, group, whole),
        grid_spec=pltpu.PrefetchScalarGridSpec(
            num_scalar_prefetch=1,
            grid=(len(group),),
            in_specs=in_specs,
            out_specs=out_specs,
            scratch_shapes=[
                pltpu.VMEM((depth // 128, lines * width, 128), F32),
                pltpu.VMEM((copies * lines, 2 * lines), BF16),
                pltpu.VMEM((plan.parts, 16, depth), F32),
            ],
        ),
        out_shape=out_shape,
        compiler_params=pltpu.CompilerParams(vmem_limit_bytes=VMEM_LIMIT),
        cost_estimate=pl.CostEstimate(
            flops=700_000_000 * len(group),
            transcendentals=0,
            bytes_accessed=17_000_000 * len(group),
        ),
        name="advance_lines",
    )(*args)
    count = pieces(plan, whole)
    return results[:count], results[count:]


def result_kernel(plan, me_ref, shift_ref, successor_ref, *refs):
    sources, refs = blockwise(plan, refs)
    follower_ref, out_ref, speed = refs[:3]
    scales = refs[3:]
    row = pl.program_id(0)

    @pl.when(row == 0)
    def _():
        prepare(plan, sources, scales)

    receive(plan, me_ref[0], row, sources, scales, speed)
    for c in range(3):
        out_ref[c, 0] = pltpu.roll(speed[c], shift_ref[0], axis=1) - follower_ref[0, c, 0]


def result(plan, me, shift, successor, blocks, tangents):
    parts = plan.parts
    block = (3, 1, plan.nx, plan.nz)
    return pl.pallas_call(
        functools.partial(result_kernel, plan),
        grid_spec=pltpu.PrefetchScalarGridSpec(
            num_scalar_prefetch=3,
            grid=(plan.rows,),
            in_specs=whole_blocks(plan)
            + [
                pl.BlockSpec(
                    (1, *block), lambda j, me, shift, successor: (successor[0], 0, j, 0, 0)
                )
            ],
            out_specs=pl.BlockSpec(block, lambda j, *_: (0, j, 0, 0)),
            scratch_shapes=[pltpu.VMEM((3, plan.nx, plan.nz), F32)]
            + [pltpu.VMEM((parts, 16, plan.depth), F32)] * len(GROUPS),
        ),
        out_shape=jax.ShapeDtypeStruct((3, plan.rows, plan.nx, plan.nz), F32),
        compiler_params=pltpu.CompilerParams(vmem_limit_bytes=VMEM_LIMIT),
        cost_estimate=pl.CostEstimate(flops=0, transcendentals=0, bytes_accessed=25_000_000),
        name="result",
    )(me, shift, successor, *flat(blocks), tangents)


def exchange(plan, whole, blocks):
    if whole:
        return [lax.all_to_all(blocks[0], "grid", split_axis=0, concat_axis=0, tiled=True)]
    parts = plan.parts
    moved = list(blocks)
    half = parts // 2
    order = [half // 2, *range(half, parts)] + [d for d in range(1, half) if d != half // 2][::-1]
    for d in order:
        moved[d] = lax.ppermute(blocks[d], "grid", [(i, i ^ d) for i in range(parts)])
    return moved


def shards(
    tangent, base_flow, base_shear, wall_derivative, implicit_inverse, successor, spanwise_shift
):
    tangent, flow, shear = tangent[0], base_flow[0], base_shear[0]
    _, rows, nx, nz = tangent.shape
    plan = Plan(rows, nx, nz, lax.axis_size("grid"))
    me = lax.axis_index("grid").astype(jnp.int32).reshape(1)
    ahead = lax.dynamic_slice_in_dim(successor, lax.axis_index("seg"), 1)
    dx = jnp.asarray(np.concatenate(halves(spectral_table(nx)), axis=0))
    dz = jnp.asarray(np.stack(halves(spectral_table(nz).T)))

    start = pack_start(plan, tangent, flow)
    later, start, following = lax.optimization_barrier((me, start, tangent))
    tangents = lax.all_gather(following, "seg")
    (start,) = exchange(plan, True, [start])
    term, bases = zip(
        *(explicit(plan, i, later, tangent, flow, shear, dx, dz) for i in range(len(WHOLE)))
    )
    right, turned, wall_flow = first_lines(plan, start, wall_derivative)
    states = [(right, turned) for _ in GROUPS]
    for section in range(SECTIONS):
        value = []
        for g, (whole, group) in enumerate(zip(WHOLE, GROUPS)):
            blocks, states[g] = advance_lines(
                plan,
                section,
                group,
                whole,
                me,
                term,
                wall_derivative,
                implicit_inverse,
                *(states[g] if section < SECTIONS - 1 else (states[g][0], None)),
                wall_flow,
            )
            value.append(exchange(plan, whole, blocks))
        if section < SECTIONS - 1:
            term = [
                explicit(plan, i, me, value, flow, shear, dx, dz, bases[i])[0]
                for i in range(len(WHOLE))
            ]
    return result(plan, me, spanwise_shift, ahead, value, tangents)[None]


def solution(mesh):
    placed = P("seg", None, "grid", None, None)
    return jax.shard_map(
        shards,
        mesh=mesh,
        in_specs=(placed, placed, placed, P(), P(), P(), P("seg")),
        out_specs=placed,
        check_vma=False,
    )
```

```python
import functools

import numpy as np
import jax
import jax.numpy as jnp
from jax import lax
from jax.experimental import pallas as pl
from jax.experimental.pallas import tpu as pltpu
from jax.sharding import PartitionSpec as P

TIME_STEP = 0.05
GAMMAS = (8.0 / 15.0, 5.0 / 12.0, 3.0 / 4.0)
ZETAS = (0.0, -17.0 / 60.0, -5.0 / 12.0)
SECTIONS = 3
WHOLE = (True, False)
GROUPS = ((0,), (1, 2))
TOP = 32767.0
STEPS_PER_OCTAVE = 64.0
F32 = jnp.float32
BF16 = jnp.bfloat16
VMEM_LIMIT = 60 * 1024 * 1024


def spectral_table(points):
    offset = np.arange(points)[:, None] - np.arange(points)[None, :]
    away = np.where(offset == 0, 1, offset)
    table = 0.5 * (1 - 2 * (offset % 2)) / np.tan(np.pi * away / points)
    return np.where(offset == 0, 0.0, table).astype(np.float32)


def halves(table):
    high = table.astype(jnp.bfloat16)
    low = (table - high.astype(np.float32)).astype(jnp.bfloat16)
    return np.asarray(high), np.asarray(low)


def split(value):
    high = value.astype(BF16)
    return high, (value - high.astype(F32)).astype(BF16)


def dot(left, right):
    return jnp.dot(left, right, preferred_element_type=F32)


def aligned(value, multiple):
    return value if isinstance(value, int) else pl.multiple_of(value, multiple)


def partner(whole, me, d):
    return d if whole else me ^ d


class Plan:
    def __init__(self, rows, nx, nz, parts):
        self.rows, self.nx, self.nz, self.parts = rows, nx, nz, parts
        self.cuts = 1 if nx // parts >= 16 else 2
        self.width = nx * self.cuts // parts
        self.depth = nz // self.cuts
        self.lines = rows * parts
        self.scale_rows = -(-rows // 16) * 16
        early = max(rows // 4, 1)
        self.early, self.late = early, rows - early

    def rows_of(self, fields, rows=None):
        return fields * (rows or self.rows) * self.width

    def piece(self, number):
        along = aligned(number // self.cuts * self.width, self.width)
        if self.cuts == 1:
            return pl.ds(along, self.width), pl.ds(0, self.depth)
        across = aligned(number % self.cuts * self.depth, self.depth)
        return pl.ds(along, self.width), pl.ds(across, self.depth)


def scale_code(largest):
    return jnp.floor(jnp.log2(jnp.maximum(largest, 1e-35)) * STEPS_PER_OCTAVE) + 2.0


def encode(code):
    return TOP * jnp.exp2(code * (-1.0 / STEPS_PER_OCTAVE))


def decode(code):
    return (1.0 / TOP) * jnp.exp2(code * (1.0 / STEPS_PER_OCTAVE))


def to_short(value):
    return jnp.round(value).astype(jnp.int32).astype(jnp.int16)


def from_short(value):
    return value.astype(jnp.int32).astype(F32)


def column_max(values):
    return functools.reduce(
        jnp.maximum, [jnp.max(jnp.abs(v), axis=0, keepdims=True) for v in values]
    )


def pack_kernel(plan, tangent_ref, flow_ref, out_ref, codes):
    row = pl.program_id(0)
    for d in range(plan.parts):
        along, across = plan.piece(d)
        values = [tangent_ref[c, 0, along, across] for c in range(3)]
        values.append(flow_ref[0, 0, along, across].astype(F32))
        for first, group in ((0, values[:3]), (3, values[3:])):
            code = scale_code(column_max(group))
            factor = encode(code)
            for k, value in enumerate(group):
                start = pl.multiple_of(((first + k) * plan.rows + row) * plan.width, plan.width)
                out_ref[d, pl.ds(start, plan.width), :] = to_short(value * factor)
            base = 0 if first == 0 else plan.scale_rows
            codes[d, pl.ds(base + row, 1), :] = code

    @pl.when(row == plan.rows - 1)
    def _():
        for d in range(plan.parts):
            out_ref[d, plan.rows_of(4) :, :] = codes[d].astype(jnp.int32).astype(jnp.int16)


def pack_start(plan, tangent, flow):
    shape = (plan.parts, plan.rows_of(4) + 2 * plan.scale_rows, plan.depth)
    return pl.pallas_call(
        functools.partial(pack_kernel, plan),
        grid=(plan.rows,),
        in_specs=[
            pl.BlockSpec((3, 1, plan.nx, plan.nz), lambda j: (0, j, 0, 0)),
            pl.BlockSpec((1, 1, plan.nx, plan.nz), lambda j: (1, j, 0, 0)),
        ],
        out_specs=pl.BlockSpec(shape, lambda j: (0, 0, 0)),
        scratch_shapes=[pltpu.VMEM((plan.parts, 2 * plan.scale_rows, plan.depth), F32)],
        out_shape=jax.ShapeDtypeStruct(shape, jnp.int16),
        compiler_params=pltpu.CompilerParams(vmem_limit_bytes=VMEM_LIMIT),
        cost_estimate=pl.CostEstimate(flops=0, transcendentals=0, bytes_accessed=20_000_000),
        name="pack_start",
    )(tangent, flow)


def pieces(plan, whole):
    return 1 if whole else plan.parts


def each(plan, whole, refs):
    return [refs[0].at[d] for d in range(plan.parts)] if whole else list(refs)


def block_specs(plan, whole, rows, depth, index, **more):
    if whole:
        return [pl.BlockSpec((plan.parts, rows, depth), lambda i, *_: (0, index(i), 0), **more)]
    return [pl.BlockSpec((rows, depth), lambda i, *_: (index(i), 0), **more)] * plan.parts


def block_shapes(plan, whole, rows):
    shape = (plan.parts, rows, plan.depth) if whole else (rows, plan.depth)
    return [jax.ShapeDtypeStruct(shape, jnp.int16)] * pieces(plan, whole)


def flat(groups):
    return [block for blocks in groups for block in blocks]


def grouped(plan, refs):
    lists = []
    for whole in WHOLE:
        count = pieces(plan, whole)
        lists.append(refs[:count])
        refs = refs[count:]
    return lists, refs


def receive(plan, me, row, sources, scales, speed):
    for whole, group, blocks, factors in zip(WHOLE, GROUPS, sources, scales):
        for d in range(plan.parts):
            along, across = plan.piece(partner(whole, me, d))
            for k, c in enumerate(group):
                start = pl.multiple_of((k * plan.rows + row) * plan.width, plan.width)
                value = from_short(blocks[d][pl.ds(start, plan.width), :])
                speed[c, along, across] = value * factors[d, k : k + 1, :]


def prepare(plan, sources, scales):
    for group, blocks, factors in zip(GROUPS, sources, scales):
        for d in range(plan.parts):
            factors[d] = decode(from_short(blocks[d][plan.rows_of(len(group)) :, :]))


def blockwise(plan, refs):
    lists, rest = grouped(plan, refs)
    return [each(plan, whole, blocks) for whole, blocks in zip(WHOLE, lists)], rest


def explicit_kernel(plan, late, received, me_ref, *refs):
    parts, nx = plan.parts, plan.nx
    if received:
        sources, refs = blockwise(plan, refs)
    else:
        tangent_ref, refs = refs[0], refs[1:]
    flow_ref, shear_ref, dx_ref, dz_ref = refs[:4]
    refs = refs[4:]
    if received:
        base_dx_ref, base_dz_ref, refs = refs[0], refs[1], refs[2:]
    if late:
        above, rows, whole, groups = plan.early, plan.late, False, GROUPS
    else:
        above, rows, whole, groups = 0, plan.early, True, ((0, 1, 2),)
    outs = []
    for _ in groups:
        count = pieces(plan, whole)
        outs.append(each(plan, whole, refs[:count]))
        refs = refs[count:]
    if not received:
        base_dx_ref, base_dz_ref, refs = refs[0], refs[1], refs[2:]
    speed, term, codes = refs[:3]
    scales = refs[3:]
    row = pl.program_id(0)
    me = me_ref[0]
    if received:

        @pl.when(row == 0)
        def _():
            prepare(plan, sources, scales)

        receive(plan, me, above + row, sources, scales, speed)
    else:
        for c in range(3):
            speed[c] = tangent_ref[c, 0]
    for c in range(3):
        if not received:
            flow = flow_ref[c, 0]
            both = dot(dx_ref[...], flow)
            base_dx_ref[c, 0] = both[:nx] + both[nx:]
            base_dz_ref[c, 0] = dot(flow, dz_ref[0]) + dot(flow, dz_ref[1])
        high, low = split(speed[c])
        both = dot(dx_ref[...], high)
        along_x = both[:nx] + both[nx:] + dot(dx_ref[:nx, :], low)
        along_z = dot(high, dz_ref[0]) + (dot(low, dz_ref[0]) + dot(high, dz_ref[1]))
        carried = flow_ref[0, 0].astype(F32) * along_x + flow_ref[2, 0].astype(F32) * along_z
        sheared = (
            speed[0] * base_dx_ref[c, 0]
            + speed[1] * shear_ref[c, 0].astype(F32)
            + speed[2] * base_dz_ref[c, 0]
        )
        term[c] = -(carried + sheared)
    for d in range(parts):
        along, across = plan.piece(partner(whole, me, d))
        values = [term[c, along, across] for c in range(3)]
        code = scale_code(column_max(values))
        factor = encode(code)
        for group, blocks in zip(groups, outs):
            for k, c in enumerate(group):
                start = pl.multiple_of((k * rows + row) * plan.width, plan.width)
                blocks[d][pl.ds(start, plan.width), :] = to_short(values[c] * factor)
        codes[d, pl.ds(row, 1), :] = code

    @pl.when(row == rows - 1)
    def _():
        for d in range(parts):
            shorts = codes[d].astype(jnp.int32).astype(jnp.int16)
            outs[0][d][plan.rows_of(len(groups[0]), rows) :, :] = shorts


def whole_blocks(plan):
    specs = []
    for whole, group in zip(WHOLE, GROUPS):
        height = plan.rows_of(len(group)) + 16
        once = dict(pipeline_mode=pl.Buffered(1))
        specs += block_specs(plan, whole, height, plan.depth, lambda j: 0, **once)
    return specs


def explicit(plan, late, me, velocity, flow, shear, dx, dz, bases=None):
    received = bases is not None
    parts = plan.parts
    if late:
        above, rows, whole = plan.early, plan.late, False
        heights = [plan.rows_of(len(group), rows) for group in GROUPS]
    else:
        above, rows, whole, heights = 0, plan.early, True, [plan.rows_of(3, plan.early)]
    heights[0] += plan.scale_rows
    block = (3, 1, plan.nx, plan.nz)
    field = pl.BlockSpec(block, lambda j, *_: (0, above + j, 0, 0))
    own = pl.BlockSpec(block, lambda j, *_: (0, j, 0, 0))
    scratch = [
        pltpu.VMEM((3, plan.nx, plan.nz), F32),
        pltpu.VMEM((3, plan.nx, plan.nz), F32),
        pltpu.VMEM((parts, plan.scale_rows, plan.depth), F32),
    ]
    out_specs, out_shape = [], []
    for height in heights:
        out_specs += block_specs(plan, whole, height, plan.depth, lambda j: 0)
        out_shape += block_shapes(plan, whole, height)
    if received:
        first, more = whole_blocks(plan), [own, own]
        velocity = flat(velocity)
        scratch += [pltpu.VMEM((parts, 16, plan.depth), F32)] * len(GROUPS)
    else:
        first, velocity, bases, more = [field], [velocity], [], []
        out_specs += [own, own]
        out_shape += [jax.ShapeDtypeStruct((3, rows, plan.nx, plan.nz), F32)] * 2
    results = pl.pallas_call(
        functools.partial(explicit_kernel, plan, late, received),
        grid_spec=pltpu.PrefetchScalarGridSpec(
            num_scalar_prefetch=1,
            grid=(rows,),
            in_specs=first
            + [
                field,
                field,
                pl.BlockSpec(dx.shape, lambda j, *_: (0, 0)),
                pl.BlockSpec(dz.shape, lambda j, *_: (0, 0, 0)),
            ]
            + more,
            out_specs=out_specs,
            scratch_shapes=scratch,
        ),
        out_shape=out_shape,
        compiler_params=pltpu.CompilerParams(vmem_limit_bytes=VMEM_LIMIT),
        cost_estimate=pl.CostEstimate(
            flops=1_000_000_000 * rows, transcendentals=0, bytes_accessed=4_000_000 * rows
        ),
        name="explicit",
    )(me, *velocity, flow, shear, dx, dz, *bases)
    count = pieces(plan, whole)
    blocks = [list(results[i * count : (i + 1) * count]) for i in range(len(heights))]
    return blocks, results[count * len(heights) :]


def stacked(matrices):
    rows = []
    for matrix in matrices:
        high, low = split(matrix)
        rows.append(jnp.concatenate([high, high], axis=1))
        rows.append(jnp.concatenate([low, jnp.zeros_like(low)], axis=1))
    return jnp.concatenate(rows, axis=0)


def precise_dot(left, right):
    high, low = split(left)
    right_high, right_low = split(right)
    return dot(high, right_high) + (dot(low, right_high) + dot(high, right_low))


def put(field, rows, value):
    for half in range(field.shape[0]):
        field[half, rows, :] = value[:, half * 128 : half * 128 + 128]


def get(field, rows):
    return jnp.concatenate([field[half, rows, :] for half in range(field.shape[0])], axis=1)


def unpack_lines(plan, whole, me, span, sources, scales, field):
    above, rows = span
    for d, (source, scale) in enumerate(zip(sources, scales)):
        scale = decode(from_short(scale[...]))
        first = aligned(partner(whole, me, d) * plan.rows_of(1), plan.width)
        for j in range(rows):
            value = from_short(source[j * plan.width : (j + 1) * plan.width, :])
            here = pl.ds(first + (above + j) * plan.width, plan.width)
            put(field, here, value * scale[j : j + 1, :])


def first_lines_kernel(plan, *refs):
    lines = plan.lines
    values, scales, flows, flow_scales = (each(plan, True, refs[i : i + 1]) for i in range(4))
    wall_ref, right_ref, turned_ref, flow_ref, field, table = refs[4:]

    @pl.when(pl.program_id(0) == 0)
    def _():
        table[...] = stacked([wall_ref[...]])
        unpack_lines(plan, True, None, (0, plan.rows), flows, flow_scales, field)

        def turn(r, carry):
            flow_ref[r] = get(field, pl.ds(r, lines, stride=plan.width))
            return carry

        lax.fori_loop(0, plan.width, turn, 0)

    unpack_lines(plan, True, None, (0, plan.rows), values, scales, field)

    def line(r, carry):
        value = get(field, pl.ds(r, lines, stride=plan.width))
        product = dot(table[...], jnp.concatenate(split(value), axis=0))
        turned = -(flow_ref[r] * (product[:lines] + product[lines:]))
        turned_ref[0, r] = turned
        right_ref[0, r] = value + (TIME_STEP * GAMMAS[0]) * turned
        return carry

    lax.fori_loop(0, plan.width, line, 0, unroll=4)


def first_lines(plan, blocks, wall):
    lines, width, depth = plan.lines, plan.width, plan.depth
    at = plan.rows_of(4) // plan.scale_rows
    rows, codes = plan.rows_of(1), plan.scale_rows
    state = jax.ShapeDtypeStruct((3, width, lines, depth), F32)
    state_spec = pl.BlockSpec((1, width, lines, depth), lambda c: (c, 0, 0, 0))
    return pl.pallas_call(
        functools.partial(first_lines_kernel, plan),
        grid=(3,),
        in_specs=block_specs(plan, True, rows, depth, lambda c: c)
        + block_specs(plan, True, codes, depth, lambda c: at)
        + block_specs(plan, True, rows, depth, lambda c: 3)
        + block_specs(plan, True, codes, depth, lambda c: at + 1)
        + [pl.BlockSpec(wall.shape, lambda c: (0, 0))],
        out_specs=[
            state_spec,
            state_spec,
            pl.BlockSpec((width, lines, depth), lambda c: (0, 0, 0)),
        ],
        scratch_shapes=[
            pltpu.VMEM((depth // 128, lines * width, 128), F32),
            pltpu.VMEM((2 * lines, 2 * lines), BF16),
        ],
        out_shape=[state, state, jax.ShapeDtypeStruct((width, lines, depth), F32)],
        compiler_params=pltpu.CompilerParams(vmem_limit_bytes=VMEM_LIMIT),
        cost_estimate=pl.CostEstimate(
            flops=1_000_000_000, transcendentals=0, bytes_accessed=30_000_000
        ),
        name="first_lines",
    )(blocks, blocks, blocks, blocks, wall)


def lines_kernel(plan, section, group, whole, me_ref, *refs):
    parts, lines = plan.parts, plan.lines
    last = section == SECTIONS - 1
    count = pieces(plan, whole)
    values, refs = blockwise(plan, refs)
    scales, refs = blockwise(plan, refs)
    if last:
        wall_ref, solve_ref, right_ref = refs[:3]
        outs, (field, table, codes) = refs[3 : 3 + count], refs[3 + count :]
    else:
        wall_ref, solve_ref, right_ref, turned_ref, flow_ref = refs[:5]
        outs, refs = refs[5 : 5 + count], refs[5 + count :]
        right_out, turned_out, field, table, codes = refs
    outs = each(plan, whole, outs)
    me = me_ref[0]
    component = pl.program_id(0)

    @pl.when(component == 0)
    def _():
        solve = solve_ref[0]
        tables = [solve] if last else [solve, precise_dot(wall_ref[...], solve)]
        table[...] = stacked(tables)
        codes[...] = jnp.zeros_like(codes)

    spans = ((0, plan.early), (plan.early, plan.late))
    for kind, span, blocks, codings in zip((True, False), spans, values, scales):
        unpack_lines(plan, kind, me, span, blocks, codings, field)

    def line(r, carry):
        here = pl.ds(r, lines, stride=plan.width)
        term = get(field, here)
        right = right_ref[0, r] + (TIME_STEP * GAMMAS[section]) * term
        product = dot(table[...], jnp.concatenate(split(right), axis=0))
        value = product[:lines] + product[lines : 2 * lines]
        put(field, here, value)
        if not last:
            slope = product[2 * lines : 3 * lines] + product[3 * lines :]
            turned = -(flow_ref[r] * slope)
            past = term + turned_ref[0, r]
            turned_out[0, r] = turned
            right_out[0, r] = (
                value
                + (TIME_STEP * ZETAS[section + 1]) * past
                + (TIME_STEP * GAMMAS[section + 1]) * turned
            )
        return carry

    lax.fori_loop(0, plan.width, line, 0, unroll=4)

    for d in range(parts):
        first = aligned(partner(whole, me, d) * plan.rows_of(1), plan.width)
        chunk = [
            get(field, pl.ds(first + j * plan.width, plan.width)) for j in range(plan.rows)
        ]
        code = scale_code(column_max(chunk))
        factor = encode(code)
        for j in range(plan.rows):
            start = pl.multiple_of((component * plan.rows + j) * plan.width, plan.width)
            outs[d][pl.ds(start, plan.width), :] = to_short(chunk[j] * factor)
        codes[d, pl.ds(component, 1), :] = code

    @pl.when(component == len(group) - 1)
    def _():
        for d in range(parts):
            outs[d][plan.rows_of(len(group)) :, :] = codes[d].astype(jnp.int32).astype(jnp.int16)


def advance_lines(plan, section, group, whole, me, blocks, wall, solves, right, turned, flow):
    lines, width, depth = plan.lines, plan.width, plan.depth
    last = section == SECTIONS - 1
    height = plan.rows_of(len(group)) + 16
    skip = group[0] if right.shape[0] == 3 else 0
    early, first_late, late = blocks
    early_at = plan.rows_of(3, plan.early) // plan.scale_rows
    late_at = plan.rows_of(len(GROUPS[0]), plan.late) // plan.scale_rows
    rows = plan.rows_of(1, plan.early), plan.rows_of(1, plan.late)
    value_specs = block_specs(plan, True, rows[0], depth, lambda c: c + group[0])
    value_specs += block_specs(plan, False, rows[1], depth, lambda c: c)
    scale_specs = block_specs(plan, True, plan.scale_rows, depth, lambda c: early_at)
    scale_specs += block_specs(plan, False, plan.scale_rows, depth, lambda c: late_at)
    state_spec = pl.BlockSpec((1, width, lines, depth), lambda c, *_: (c, 0, 0, 0))
    read_spec = pl.BlockSpec((1, width, lines, depth), lambda c, *_: (c + skip, 0, 0, 0))
    in_specs = (
        value_specs
        + scale_specs
        + [
            pl.BlockSpec(wall.shape, lambda c, *_: (0, 0)),
            pl.BlockSpec((1, lines, lines), lambda c, *_: (section, 0, 0)),
            read_spec,
        ]
    )
    args = [me, *early, *late, *early, *first_late, wall, solves, right]
    out_specs = block_specs(plan, whole, height, depth, lambda c: 0)
    out_shape = block_shapes(plan, whole, height)
    copies = 2
    if not last:
        in_specs += [
            read_spec,
            pl.BlockSpec(flow.shape, lambda c, *_: (0, 0, 0), pipeline_mode=pl.Buffered(1)),
        ]
        args += [turned, flow]
        out_specs = out_specs + [state_spec, state_spec]
        state = jax.ShapeDtypeStruct((len(group), width, lines, depth), F32)
        out_shape = out_shape + [state, state]
        copies = 4
    results = pl.pallas_call(
        functools.partial(lines_kernel, plan, section, group, whole),
        grid_spec=pltpu.PrefetchScalarGridSpec(
            num_scalar_prefetch=1,
            grid=(len(group),),
            in_specs=in_specs,
            out_specs=out_specs,
            scratch_shapes=[
                pltpu.VMEM((depth // 128, lines * width, 128), F32),
                pltpu.VMEM((copies * lines, 2 * lines), BF16),
                pltpu.VMEM((plan.parts, 16, depth), F32),
            ],
        ),
        out_shape=out_shape,
        compiler_params=pltpu.CompilerParams(vmem_limit_bytes=VMEM_LIMIT),
        cost_estimate=pl.CostEstimate(
            flops=700_000_000 * len(group),
            transcendentals=0,
            bytes_accessed=17_000_000 * len(group),
        ),
        name="advance_lines",
    )(*args)
    count = pieces(plan, whole)
    return results[:count], results[count:]


def result_kernel(plan, group, whole, me_ref, shift_ref, successor_ref, *refs):
    count = pieces(plan, whole)
    blocks, refs = each(plan, whole, refs[:count]), refs[count:]
    follower_ref, (out_ref, speed, factors) = refs[0], refs[-3:]
    component, row = pl.program_id(0), pl.program_id(1)

    @pl.when((component == 0) & (row == 0))
    def _():
        for d in range(plan.parts):
            factors[d] = decode(from_short(blocks[d][plan.rows_of(len(group)) :, :]))

    for d in range(plan.parts):
        along, across = plan.piece(partner(whole, me_ref[0], d))
        start = pl.multiple_of((component * plan.rows + row) * plan.width, plan.width)
        value = from_short(blocks[d][pl.ds(start, plan.width), :])
        speed[along, across] = value * factors[d, pl.ds(component, 1), :]
    rolled = pltpu.roll(speed[...], shift_ref[0], axis=1)
    out_ref[0, 0] = rolled - follower_ref[0, 0, 0]


def result(plan, group, whole, me, shift, successor, blocks, tangents, before):
    height = plan.rows_of(len(group)) + 16
    specs = block_specs(
        plan, whole, height, plan.depth, lambda c: 0, pipeline_mode=pl.Buffered(1)
    )
    specs.append(
        pl.BlockSpec(
            (1, 1, 1, plan.nx, plan.nz),
            lambda c, j, me, shift, successor: (successor[0], c + group[0], j, 0, 0),
        )
    )
    args = [me, shift, successor, *blocks, tangents]
    aliases = {}
    if before is not None:
        specs.append(pl.BlockSpec(memory_space=pl.ANY))
        aliases[len(args)] = 0
        args.append(before)
    return pl.pallas_call(
        functools.partial(result_kernel, plan, group, whole),
        grid_spec=pltpu.PrefetchScalarGridSpec(
            num_scalar_prefetch=3,
            grid=(len(group), plan.rows),
            in_specs=specs,
            out_specs=pl.BlockSpec(
                (1, 1, plan.nx, plan.nz), lambda c, j, *_: (c + group[0], j, 0, 0)
            ),
            scratch_shapes=[
                pltpu.VMEM((plan.nx, plan.nz), F32),
                pltpu.VMEM((plan.parts, 16, plan.depth), F32),
            ],
        ),
        out_shape=jax.ShapeDtypeStruct((3, plan.rows, plan.nx, plan.nz), F32),
        input_output_aliases=aliases,
        compiler_params=pltpu.CompilerParams(vmem_limit_bytes=VMEM_LIMIT),
        cost_estimate=pl.CostEstimate(
            flops=0, transcendentals=0, bytes_accessed=8_000_000 * len(group)
        ),
        name="result",
    )(*args)


def exchange(plan, whole, blocks):
    if whole:
        return [lax.all_to_all(blocks[0], "grid", split_axis=0, concat_axis=0, tiled=True)]
    parts = plan.parts
    moved = list(blocks)
    half = parts // 2
    order = [half // 2, *range(half, parts)] + [d for d in range(1, half) if d != half // 2][::-1]
    for d in order:
        moved[d] = lax.ppermute(blocks[d], "grid", [(i, i ^ d) for i in range(parts)])
    return moved


def shards(
    tangent, base_flow, base_shear, wall_derivative, implicit_inverse, successor, spanwise_shift
):
    tangent, flow, shear = tangent[0], base_flow[0], base_shear[0]
    _, rows, nx, nz = tangent.shape
    plan = Plan(rows, nx, nz, lax.axis_size("grid"))
    me = lax.axis_index("grid").astype(jnp.int32).reshape(1)
    ahead = lax.dynamic_slice_in_dim(successor, lax.axis_index("seg"), 1)
    dx = jnp.asarray(np.concatenate(halves(spectral_table(nx)), axis=0))
    dz = jnp.asarray(np.stack(halves(spectral_table(nz).T)))

    start = pack_start(plan, tangent, flow)
    later, start, following = lax.optimization_barrier((me, start, tangent))
    tangents = lax.all_gather(following, "seg")
    (start,) = exchange(plan, True, [start])
    bases = []
    early, base = explicit(plan, False, later, tangent, flow, shear, dx, dz)
    bases.append(base)
    late, base = explicit(plan, True, later, tangent, flow, shear, dx, dz)
    bases.append(base)
    early[0][0], late[0][0] = lax.optimization_barrier((early[0][0], late[0][0]))
    term = [exchange(plan, True, early[0]), [exchange(plan, False, blocks) for blocks in late]]
    right, turned, wall_flow = first_lines(plan, start, wall_derivative)
    states = [(right, turned) for _ in GROUPS]
    for section in range(SECTIONS):
        value = []
        for g, (whole, group) in enumerate(zip(WHOLE, GROUPS)):
            blocks, states[g] = advance_lines(
                plan,
                section,
                group,
                whole,
                me,
                [term[0], term[1][0], term[1][g]],
                wall_derivative,
                implicit_inverse,
                *(states[g] if section < SECTIONS - 1 else (states[g][0], None)),
                wall_flow,
            )
            if g == 0:
                blocks, term[1][1] = lax.optimization_barrier((blocks, term[1][1]))
            value.append(exchange(plan, whole, blocks))
        if section < SECTIONS - 1:
            early, _ = explicit(plan, False, me, value, flow, shear, dx, dz, bases[0])
            early = exchange(plan, True, early[0])
            late, _ = explicit(plan, True, me, value, flow, shear, dx, dz, bases[1])
            term = [early, [exchange(plan, False, blocks) for blocks in late]]
    out = None
    for group, whole, blocks in zip(GROUPS, WHOLE, value):
        out = result(plan, group, whole, me, spanwise_shift, ahead, blocks, tangents, out)
    return out[None]


def solution(mesh):
    placed = P("seg", None, "grid", None, None)
    return jax.shard_map(
        shards,
        mesh=mesh,
        in_specs=(placed, placed, placed, P(), P(), P(), P("seg")),
        out_specs=placed,
        check_vma=False,
    )
```

```python
import functools

import numpy as np
import jax
import jax.numpy as jnp
from jax import lax
from jax.experimental import pallas as pl
from jax.experimental.pallas import tpu as pltpu
from jax.sharding import PartitionSpec as P

TIME_STEP = 0.05
GAMMAS = (8.0 / 15.0, 5.0 / 12.0, 3.0 / 4.0)
ZETAS = (0.0, -17.0 / 60.0, -5.0 / 12.0)
SECTIONS = 3
WHOLE = (True, False)
GROUPS = ((0,), (1, 2))
TOP = 32767.0
STEPS_PER_OCTAVE = 64.0
F32 = jnp.float32
BF16 = jnp.bfloat16
VMEM_LIMIT = 60 * 1024 * 1024


def spectral_table(points):
    offset = np.arange(points)[:, None] - np.arange(points)[None, :]
    away = np.where(offset == 0, 1, offset)
    table = 0.5 * (1 - 2 * (offset % 2)) / np.tan(np.pi * away / points)
    return np.where(offset == 0, 0.0, table).astype(np.float32)


def halves(table):
    high = table.astype(jnp.bfloat16)
    low = (table - high.astype(np.float32)).astype(jnp.bfloat16)
    return np.asarray(high), np.asarray(low)


def split(value):
    high = value.astype(BF16)
    return high, (value - high.astype(F32)).astype(BF16)


def dot(left, right):
    return jnp.dot(left, right, preferred_element_type=F32)


def aligned(value, multiple):
    return value if isinstance(value, int) else pl.multiple_of(value, multiple)


def bits_of(parts):
    half = parts // 2
    far = list(range(half, parts))
    near = [d for d in range(1, half) if d != half // 2][::-1]
    return [0, half // 2, *far, *near] if parts > 2 else list(range(parts))


def partner(plan, whole, me, d):
    return d if whole else me ^ plan.bits[d]


class Plan:
    def __init__(self, rows, nx, nz, parts):
        self.rows, self.nx, self.nz, self.parts = rows, nx, nz, parts
        self.cuts = 1 if nx // parts >= 16 else 2
        self.width = nx * self.cuts // parts
        self.depth = nz // self.cuts
        self.lines = rows * parts
        self.bits = bits_of(parts)
        self.scale_rows = -(-rows // 16) * 16
        early = max(rows // 4, 1)
        self.early, self.late = early, rows - early

    def rows_of(self, fields, rows=None):
        return fields * (rows or self.rows) * self.width

    def piece(self, number):
        along = aligned(number // self.cuts * self.width, self.width)
        if self.cuts == 1:
            return pl.ds(along, self.width), pl.ds(0, self.depth)
        across = aligned(number % self.cuts * self.depth, self.depth)
        return pl.ds(along, self.width), pl.ds(across, self.depth)


def scale_code(largest):
    return jnp.floor(jnp.log2(jnp.maximum(largest, 1e-35)) * STEPS_PER_OCTAVE) + 2.0


def encode(code):
    return TOP * jnp.exp2(code * (-1.0 / STEPS_PER_OCTAVE))


def decode(code):
    return (1.0 / TOP) * jnp.exp2(code * (1.0 / STEPS_PER_OCTAVE))


def to_short(value):
    return jnp.round(value).astype(jnp.int32).astype(jnp.int16)


def from_short(value):
    return value.astype(jnp.int32).astype(F32)


def column_max(values):
    return functools.reduce(
        jnp.maximum, [jnp.max(jnp.abs(v), axis=0, keepdims=True) for v in values]
    )


def pack_kernel(plan, tangent_ref, flow_ref, out_ref, codes):
    row = pl.program_id(0)
    for d in range(plan.parts):
        along, across = plan.piece(d)
        values = [tangent_ref[c, 0, along, across] for c in range(3)]
        values.append(flow_ref[0, 0, along, across].astype(F32))
        for first, group in ((0, values[:3]), (3, values[3:])):
            code = scale_code(column_max(group))
            factor = encode(code)
            for k, value in enumerate(group):
                start = pl.multiple_of(((first + k) * plan.rows + row) * plan.width, plan.width)
                out_ref[d, pl.ds(start, plan.width), :] = to_short(value * factor)
            base = 0 if first == 0 else plan.scale_rows
            codes[d, pl.ds(base + row, 1), :] = code

    @pl.when(row == plan.rows - 1)
    def _():
        for d in range(plan.parts):
            out_ref[d, plan.rows_of(4) :, :] = codes[d].astype(jnp.int32).astype(jnp.int16)


def pack_start(plan, tangent, flow):
    shape = (plan.parts, plan.rows_of(4) + 2 * plan.scale_rows, plan.depth)
    return pl.pallas_call(
        functools.partial(pack_kernel, plan),
        grid=(plan.rows,),
        in_specs=[
            pl.BlockSpec((3, 1, plan.nx, plan.nz), lambda j: (0, j, 0, 0)),
            pl.BlockSpec((1, 1, plan.nx, plan.nz), lambda j: (1, j, 0, 0)),
        ],
        out_specs=pl.BlockSpec(shape, lambda j: (0, 0, 0)),
        scratch_shapes=[pltpu.VMEM((plan.parts, 2 * plan.scale_rows, plan.depth), F32)],
        out_shape=jax.ShapeDtypeStruct(shape, jnp.int16),
        compiler_params=pltpu.CompilerParams(vmem_limit_bytes=VMEM_LIMIT),
        cost_estimate=pl.CostEstimate(flops=0, transcendentals=0, bytes_accessed=20_000_000),
        name="pack_start",
    )(tangent, flow)


def pieces(plan, whole):
    return 1 if whole else plan.parts


def each(plan, whole, refs):
    return [refs[0].at[d] for d in range(plan.parts)] if whole else list(refs)


def block_specs(plan, whole, rows, depth, index, **more):
    if whole:
        return [pl.BlockSpec((plan.parts, rows, depth), lambda i, *_: (0, index(i), 0), **more)]
    return [pl.BlockSpec((rows, depth), lambda i, *_: (index(i), 0), **more)] * plan.parts


def block_shapes(plan, whole, rows):
    shape = (plan.parts, rows, plan.depth) if whole else (rows, plan.depth)
    return [jax.ShapeDtypeStruct(shape, jnp.int16)] * pieces(plan, whole)


def flat(groups):
    return [block for blocks in groups for block in blocks]


def grouped(plan, refs):
    lists = []
    for whole in WHOLE:
        count = pieces(plan, whole)
        lists.append(refs[:count])
        refs = refs[count:]
    return lists, refs


def receive(plan, me, row, sources, scales, speed):
    for whole, group, blocks, factors in zip(WHOLE, GROUPS, sources, scales):
        for d in range(plan.parts):
            along, across = plan.piece(partner(plan, whole, me, d))
            for k, c in enumerate(group):
                start = pl.multiple_of((k * plan.rows + row) * plan.width, plan.width)
                value = from_short(blocks[d][pl.ds(start, plan.width), :])
                speed[c, along, across] = value * factors[d, k : k + 1, :]


def prepare(plan, sources, scales):
    for group, blocks, factors in zip(GROUPS, sources, scales):
        for d in range(plan.parts):
            factors[d] = decode(from_short(blocks[d][plan.rows_of(len(group)) :, :]))


def blockwise(plan, refs):
    lists, rest = grouped(plan, refs)
    return [each(plan, whole, blocks) for whole, blocks in zip(WHOLE, lists)], rest


def explicit_kernel(plan, late, received, me_ref, *refs):
    parts, nx = plan.parts, plan.nx
    if received:
        sources, refs = blockwise(plan, refs)
    else:
        tangent_ref, refs = refs[0], refs[1:]
    flow_ref, shear_ref, dx_ref, dz_ref = refs[:4]
    refs = refs[4:]
    if received:
        base_dx_ref, base_dz_ref, refs = refs[0], refs[1], refs[2:]
    if late:
        above, rows, whole, groups = plan.early, plan.late, False, GROUPS
    else:
        above, rows, whole, groups = 0, plan.early, True, ((0, 1, 2),)
    outs = []
    for _ in groups:
        count = pieces(plan, whole)
        outs.append(each(plan, whole, refs[:count]))
        refs = refs[count:]
    if not received:
        base_dx_ref, base_dz_ref, refs = refs[0], refs[1], refs[2:]
    speed, term, codes = refs[:3]
    scales = refs[3:]
    row = pl.program_id(0)
    me = me_ref[0]
    if received:

        @pl.when(row == 0)
        def _():
            prepare(plan, sources, scales)

        receive(plan, me, above + row, sources, scales, speed)
    else:
        for c in range(3):
            speed[c] = tangent_ref[c, 0]
    for c in range(3):
        if not received:
            flow = flow_ref[c, 0]
            both = dot(dx_ref[...], flow)
            base_dx_ref[c, 0] = both[:nx] + both[nx:]
            base_dz_ref[c, 0] = dot(flow, dz_ref[0]) + dot(flow, dz_ref[1])
        high, low = split(speed[c])
        both = dot(dx_ref[...], high)
        along_x = both[:nx] + both[nx:] + dot(dx_ref[:nx, :], low)
        along_z = dot(high, dz_ref[0]) + (dot(low, dz_ref[0]) + dot(high, dz_ref[1]))
        carried = flow_ref[0, 0].astype(F32) * along_x + flow_ref[2, 0].astype(F32) * along_z
        sheared = (
            speed[0] * base_dx_ref[c, 0]
            + speed[1] * shear_ref[c, 0].astype(F32)
            + speed[2] * base_dz_ref[c, 0]
        )
        term[c] = -(carried + sheared)
    for d in range(parts):
        along, across = plan.piece(partner(plan, whole, me, d))
        values = [term[c, along, across] for c in range(3)]
        code = scale_code(column_max(values))
        factor = encode(code)
        for group, blocks in zip(groups, outs):
            for k, c in enumerate(group):
                start = pl.multiple_of((k * rows + row) * plan.width, plan.width)
                blocks[d][pl.ds(start, plan.width), :] = to_short(values[c] * factor)
        codes[d, pl.ds(row, 1), :] = code

    @pl.when(row == rows - 1)
    def _():
        for d in range(parts):
            shorts = codes[d].astype(jnp.int32).astype(jnp.int16)
            outs[0][d][plan.rows_of(len(groups[0]), rows) :, :] = shorts


def whole_blocks(plan):
    specs = []
    for whole, group in zip(WHOLE, GROUPS):
        height = plan.rows_of(len(group)) + 16
        once = dict(pipeline_mode=pl.Buffered(1))
        specs += block_specs(plan, whole, height, plan.depth, lambda j: 0, **once)
    return specs


def explicit(plan, late, me, velocity, flow, shear, dx, dz, bases=None):
    received = bases is not None
    parts = plan.parts
    if late:
        above, rows, whole = plan.early, plan.late, False
        heights = [plan.rows_of(len(group), rows) for group in GROUPS]
    else:
        above, rows, whole, heights = 0, plan.early, True, [plan.rows_of(3, plan.early)]
    heights[0] += plan.scale_rows
    block = (3, 1, plan.nx, plan.nz)
    field = pl.BlockSpec(block, lambda j, *_: (0, above + j, 0, 0))
    own = pl.BlockSpec(block, lambda j, *_: (0, j, 0, 0))
    scratch = [
        pltpu.VMEM((3, plan.nx, plan.nz), F32),
        pltpu.VMEM((3, plan.nx, plan.nz), F32),
        pltpu.VMEM((parts, plan.scale_rows, plan.depth), F32),
    ]
    out_specs, out_shape = [], []
    for height in heights:
        out_specs += block_specs(plan, whole, height, plan.depth, lambda j: 0)
        out_shape += block_shapes(plan, whole, height)
    if received:
        first, more = whole_blocks(plan), [own, own]
        velocity = flat(velocity)
        scratch += [pltpu.VMEM((parts, 16, plan.depth), F32)] * len(GROUPS)
    else:
        first, velocity, bases, more = [field], [velocity], [], []
        out_specs += [own, own]
        out_shape += [jax.ShapeDtypeStruct((3, rows, plan.nx, plan.nz), F32)] * 2
    results = pl.pallas_call(
        functools.partial(explicit_kernel, plan, late, received),
        grid_spec=pltpu.PrefetchScalarGridSpec(
            num_scalar_prefetch=1,
            grid=(rows,),
            in_specs=first
            + [
                field,
                field,
                pl.BlockSpec(dx.shape, lambda j, *_: (0, 0)),
                pl.BlockSpec(dz.shape, lambda j, *_: (0, 0, 0)),
            ]
            + more,
            out_specs=out_specs,
            scratch_shapes=scratch,
        ),
        out_shape=out_shape,
        compiler_params=pltpu.CompilerParams(vmem_limit_bytes=VMEM_LIMIT),
        cost_estimate=pl.CostEstimate(
            flops=1_000_000_000 * rows, transcendentals=0, bytes_accessed=4_000_000 * rows
        ),
        name="explicit",
    )(me, *velocity, flow, shear, dx, dz, *bases)
    count = pieces(plan, whole)
    blocks = [list(results[i * count : (i + 1) * count]) for i in range(len(heights))]
    return blocks, results[count * len(heights) :]


def stacked(matrices):
    rows = []
    for matrix in matrices:
        high, low = split(matrix)
        rows.append(jnp.concatenate([high, high], axis=1))
        rows.append(jnp.concatenate([low, jnp.zeros_like(low)], axis=1))
    return jnp.concatenate(rows, axis=0)


def precise_dot(left, right):
    high, low = split(left)
    right_high, right_low = split(right)
    return dot(high, right_high) + (dot(low, right_high) + dot(high, right_low))


def put(field, rows, value):
    for half in range(field.shape[0]):
        field[half, rows, :] = value[:, half * 128 : half * 128 + 128]


def get(field, rows):
    return jnp.concatenate([field[half, rows, :] for half in range(field.shape[0])], axis=1)


def unpack_lines(plan, whole, me, span, sources, scales, field):
    above, rows = span
    for d, (source, scale) in enumerate(zip(sources, scales)):
        scale = decode(from_short(scale[...]))
        first = aligned(partner(plan, whole, me, d) * plan.rows_of(1), plan.width)
        for j in range(rows):
            value = from_short(source[j * plan.width : (j + 1) * plan.width, :])
            here = pl.ds(first + (above + j) * plan.width, plan.width)
            put(field, here, value * scale[j : j + 1, :])


def first_lines_kernel(plan, *refs):
    lines = plan.lines
    values, scales, flows, flow_scales = (each(plan, True, refs[i : i + 1]) for i in range(4))
    wall_ref, right_ref, turned_ref, flow_ref, field, table = refs[4:]

    @pl.when(pl.program_id(0) == 0)
    def _():
        table[...] = stacked([wall_ref[...]])
        unpack_lines(plan, True, None, (0, plan.rows), flows, flow_scales, field)

        def turn(r, carry):
            flow_ref[r] = get(field, pl.ds(r, lines, stride=plan.width))
            return carry

        lax.fori_loop(0, plan.width, turn, 0)

    unpack_lines(plan, True, None, (0, plan.rows), values, scales, field)

    def line(r, carry):
        value = get(field, pl.ds(r, lines, stride=plan.width))
        product = dot(table[...], jnp.concatenate(split(value), axis=0))
        turned = -(flow_ref[r] * (product[:lines] + product[lines:]))
        turned_ref[0, r] = turned
        right_ref[0, r] = value + (TIME_STEP * GAMMAS[0]) * turned
        return carry

    lax.fori_loop(0, plan.width, line, 0, unroll=4)


def first_lines(plan, blocks, wall):
    lines, width, depth = plan.lines, plan.width, plan.depth
    at = plan.rows_of(4) // plan.scale_rows
    rows, codes = plan.rows_of(1), plan.scale_rows
    state = jax.ShapeDtypeStruct((3, width, lines, depth), F32)
    state_spec = pl.BlockSpec((1, width, lines, depth), lambda c: (c, 0, 0, 0))
    return pl.pallas_call(
        functools.partial(first_lines_kernel, plan),
        grid=(3,),
        in_specs=block_specs(plan, True, rows, depth, lambda c: c)
        + block_specs(plan, True, codes, depth, lambda c: at)
        + block_specs(plan, True, rows, depth, lambda c: 3)
        + block_specs(plan, True, codes, depth, lambda c: at + 1)
        + [pl.BlockSpec(wall.shape, lambda c: (0, 0))],
        out_specs=[
            state_spec,
            state_spec,
            pl.BlockSpec((width, lines, depth), lambda c: (0, 0, 0)),
        ],
        scratch_shapes=[
            pltpu.VMEM((depth // 128, lines * width, 128), F32),
            pltpu.VMEM((2 * lines, 2 * lines), BF16),
        ],
        out_shape=[state, state, jax.ShapeDtypeStruct((width, lines, depth), F32)],
        compiler_params=pltpu.CompilerParams(vmem_limit_bytes=VMEM_LIMIT),
        cost_estimate=pl.CostEstimate(
            flops=1_000_000_000, transcendentals=0, bytes_accessed=30_000_000
        ),
        name="first_lines",
    )(blocks, blocks, blocks, blocks, wall)


def lines_kernel(plan, section, group, whole, me_ref, *refs):
    parts, lines = plan.parts, plan.lines
    last = section == SECTIONS - 1
    count = pieces(plan, whole)
    values, refs = blockwise(plan, refs)
    scales, refs = blockwise(plan, refs)
    if last:
        wall_ref, solve_ref, right_ref = refs[:3]
        outs, (field, table, codes) = refs[3 : 3 + count], refs[3 + count :]
    else:
        wall_ref, solve_ref, right_ref, turned_ref, flow_ref = refs[:5]
        outs, refs = refs[5 : 5 + count], refs[5 + count :]
        right_out, turned_out, field, table, codes = refs
    outs = each(plan, whole, outs)
    me = me_ref[0]
    component = pl.program_id(0)

    @pl.when(component == 0)
    def _():
        solve = solve_ref[0]
        tables = [solve] if last else [solve, precise_dot(wall_ref[...], solve)]
        table[...] = stacked(tables)
        codes[...] = jnp.zeros_like(codes)

    spans = ((0, plan.early), (plan.early, plan.late))
    for kind, span, blocks, codings in zip((True, False), spans, values, scales):
        unpack_lines(plan, kind, me, span, blocks, codings, field)

    def line(r, carry):
        here = pl.ds(r, lines, stride=plan.width)
        term = get(field, here)
        right = right_ref[0, r] + (TIME_STEP * GAMMAS[section]) * term
        product = dot(table[...], jnp.concatenate(split(right), axis=0))
        value = product[:lines] + product[lines : 2 * lines]
        put(field, here, value)
        if not last:
            slope = product[2 * lines : 3 * lines] + product[3 * lines :]
            turned = -(flow_ref[r] * slope)
            past = term + turned_ref[0, r]
            turned_out[0, r] = turned
            right_out[0, r] = (
                value
                + (TIME_STEP * ZETAS[section + 1]) * past
                + (TIME_STEP * GAMMAS[section + 1]) * turned
            )
        return carry

    lax.fori_loop(0, plan.width, line, 0, unroll=4)

    for d in range(parts):
        first = aligned(partner(plan, whole, me, d) * plan.rows_of(1), plan.width)
        chunk = [
            get(field, pl.ds(first + j * plan.width, plan.width)) for j in range(plan.rows)
        ]
        code = scale_code(column_max(chunk))
        factor = encode(code)
        for j in range(plan.rows):
            start = pl.multiple_of((component * plan.rows + j) * plan.width, plan.width)
            outs[d][pl.ds(start, plan.width), :] = to_short(chunk[j] * factor)
        codes[d, pl.ds(component, 1), :] = code

    @pl.when(component == len(group) - 1)
    def _():
        for d in range(parts):
            outs[d][plan.rows_of(len(group)) :, :] = codes[d].astype(jnp.int32).astype(jnp.int16)


def advance_lines(plan, section, group, whole, me, blocks, wall, solves, right, turned, flow):
    lines, width, depth = plan.lines, plan.width, plan.depth
    last = section == SECTIONS - 1
    height = plan.rows_of(len(group)) + 16
    skip = group[0] if right.shape[0] == 3 else 0
    early, first_late, late = blocks
    early_at = plan.rows_of(3, plan.early) // plan.scale_rows
    late_at = plan.rows_of(len(GROUPS[0]), plan.late) // plan.scale_rows
    rows = plan.rows_of(1, plan.early), plan.rows_of(1, plan.late)
    value_specs = block_specs(plan, True, rows[0], depth, lambda c: c + group[0])
    value_specs += block_specs(plan, False, rows[1], depth, lambda c: c)
    scale_specs = block_specs(plan, True, plan.scale_rows, depth, lambda c: early_at)
    scale_specs += block_specs(plan, False, plan.scale_rows, depth, lambda c: late_at)
    state_spec = pl.BlockSpec((1, width, lines, depth), lambda c, *_: (c, 0, 0, 0))
    read_spec = pl.BlockSpec((1, width, lines, depth), lambda c, *_: (c + skip, 0, 0, 0))
    in_specs = (
        value_specs
        + scale_specs
        + [
            pl.BlockSpec(wall.shape, lambda c, *_: (0, 0)),
            pl.BlockSpec((1, lines, lines), lambda c, *_: (section, 0, 0)),
            read_spec,
        ]
    )
    args = [me, *early, *late, *early, *first_late, wall, solves, right]
    out_specs = block_specs(plan, whole, height, depth, lambda c: 0)
    out_shape = block_shapes(plan, whole, height)
    copies = 2
    if not last:
        in_specs += [
            read_spec,
            pl.BlockSpec(flow.shape, lambda c, *_: (0, 0, 0), pipeline_mode=pl.Buffered(1)),
        ]
        args += [turned, flow]
        out_specs = out_specs + [state_spec, state_spec]
        state = jax.ShapeDtypeStruct((len(group), width, lines, depth), F32)
        out_shape = out_shape + [state, state]
        copies = 4
    results = pl.pallas_call(
        functools.partial(lines_kernel, plan, section, group, whole),
        grid_spec=pltpu.PrefetchScalarGridSpec(
            num_scalar_prefetch=1,
            grid=(len(group),),
            in_specs=in_specs,
            out_specs=out_specs,
            scratch_shapes=[
                pltpu.VMEM((depth // 128, lines * width, 128), F32),
                pltpu.VMEM((copies * lines, 2 * lines), BF16),
                pltpu.VMEM((plan.parts, 16, depth), F32),
            ],
        ),
        out_shape=out_shape,
        compiler_params=pltpu.CompilerParams(vmem_limit_bytes=VMEM_LIMIT),
        cost_estimate=pl.CostEstimate(
            flops=700_000_000 * len(group),
            transcendentals=0,
            bytes_accessed=17_000_000 * len(group),
        ),
        name="advance_lines",
    )(*args)
    count = pieces(plan, whole)
    return results[:count], results[count:]


def result_kernel(plan, group, whole, me_ref, shift_ref, successor_ref, *refs):
    count = pieces(plan, whole)
    blocks, refs = each(plan, whole, refs[:count]), refs[count:]
    follower_ref, (out_ref, speed, factors) = refs[0], refs[-3:]
    component, step = pl.program_id(0), pl.program_id(1)

    @pl.when((component == 0) & (step == 0))
    def _():
        for d in range(plan.parts):
            factors[d] = decode(from_short(blocks[d][plan.rows_of(len(group)) :, :]))

    rows = out_ref.shape[1]
    for j in range(rows):
        row = component * plan.rows + step * rows + j
        for d in range(plan.parts):
            along, across = plan.piece(partner(plan, whole, me_ref[0], d))
            start = pl.multiple_of(row * plan.width, plan.width)
            value = from_short(blocks[d][pl.ds(start, plan.width), :])
            speed[j, along, across] = value * factors[d, pl.ds(component, 1), :]
        rolled = pltpu.roll(speed[j], shift_ref[0], axis=1)
        out_ref[0, j] = rolled - follower_ref[0, 0, j]


def result(plan, group, whole, me, shift, successor, blocks, tangents, before):
    height = plan.rows_of(len(group)) + 16
    rows = next(r for r in (4, 3, 2, 1) if plan.rows % r == 0)
    specs = block_specs(
        plan, whole, height, plan.depth, lambda c: 0, pipeline_mode=pl.Buffered(1)
    )
    specs.append(
        pl.BlockSpec(
            (1, 1, rows, plan.nx, plan.nz),
            lambda c, j, me, shift, successor: (successor[0], c + group[0], j, 0, 0),
        )
    )
    args = [me, shift, successor, *blocks, tangents]
    aliases = {}
    if before is not None:
        specs.append(pl.BlockSpec(memory_space=pl.ANY))
        aliases[len(args)] = 0
        args.append(before)
    return pl.pallas_call(
        functools.partial(result_kernel, plan, group, whole),
        grid_spec=pltpu.PrefetchScalarGridSpec(
            num_scalar_prefetch=3,
            grid=(len(group), plan.rows // rows),
            in_specs=specs,
            out_specs=pl.BlockSpec(
                (1, rows, plan.nx, plan.nz), lambda c, j, *_: (c + group[0], j, 0, 0)
            ),
            scratch_shapes=[
                pltpu.VMEM((rows, plan.nx, plan.nz), F32),
                pltpu.VMEM((plan.parts, 16, plan.depth), F32),
            ],
        ),
        out_shape=jax.ShapeDtypeStruct((3, plan.rows, plan.nx, plan.nz), F32),
        input_output_aliases=aliases,
        compiler_params=pltpu.CompilerParams(vmem_limit_bytes=VMEM_LIMIT),
        cost_estimate=pl.CostEstimate(
            flops=0, transcendentals=0, bytes_accessed=8_000_000 * len(group)
        ),
        name="result",
    )(*args)


def exchange(plan, whole, blocks):
    if whole:
        return [lax.all_to_all(blocks[0], "grid", split_axis=0, concat_axis=0, tiled=True)]
    moved = list(blocks)
    for d in range(1, plan.parts):
        route = [(i, i ^ plan.bits[d]) for i in range(plan.parts)]
        moved[d] = lax.ppermute(blocks[d], "grid", route)
    return moved


def shards(
    tangent, base_flow, base_shear, wall_derivative, implicit_inverse, successor, spanwise_shift
):
    tangent, flow, shear = tangent[0], base_flow[0], base_shear[0]
    _, rows, nx, nz = tangent.shape
    plan = Plan(rows, nx, nz, lax.axis_size("grid"))
    me = lax.axis_index("grid").astype(jnp.int32).reshape(1)
    ahead = lax.dynamic_slice_in_dim(successor, lax.axis_index("seg"), 1)
    dx = jnp.asarray(np.concatenate(halves(spectral_table(nx)), axis=0))
    dz = jnp.asarray(np.stack(halves(spectral_table(nz).T)))

    start = pack_start(plan, tangent, flow)
    later, start, following = lax.optimization_barrier((me, start, tangent))
    tangents = lax.all_gather(following, "seg")
    (start,) = exchange(plan, True, [start])
    bases = []
    early, base = explicit(plan, False, later, tangent, flow, shear, dx, dz)
    bases.append(base)
    late, base = explicit(plan, True, later, tangent, flow, shear, dx, dz)
    bases.append(base)
    right, turned, wall_flow = first_lines(plan, start, wall_derivative)
    early[0][0], late = lax.optimization_barrier((early[0][0], late))
    early = exchange(plan, True, early[0])
    late, wall_flow = lax.optimization_barrier((late, wall_flow))
    term = [early, [exchange(plan, False, blocks) for blocks in late]]
    states = [(right, turned) for _ in GROUPS]
    for section in range(SECTIONS):
        value = []
        for g, (whole, group) in enumerate(zip(WHOLE, GROUPS)):
            blocks, states[g] = advance_lines(
                plan,
                section,
                group,
                whole,
                me,
                [term[0], term[1][0], term[1][g]],
                wall_derivative,
                implicit_inverse,
                *(states[g] if section < SECTIONS - 1 else (states[g][0], None)),
                wall_flow,
            )
            if g == 0:
                blocks, term[1][1] = lax.optimization_barrier((blocks, term[1][1]))
            value.append(exchange(plan, whole, blocks))
        if section < SECTIONS - 1:
            early, _ = explicit(plan, False, me, value, flow, shear, dx, dz, bases[0])
            early = exchange(plan, True, early[0])
            late, _ = explicit(plan, True, me, value, flow, shear, dx, dz, bases[1])
            term = [early, [exchange(plan, False, blocks) for blocks in late]]
    out = None
    for group, whole, blocks in zip(GROUPS, WHOLE, value):
        out = result(plan, group, whole, me, spanwise_shift, ahead, blocks, tangents, out)
    return out[None]


def solution(mesh):
    placed = P("seg", None, "grid", None, None)
    return jax.shard_map(
        shards,
        mesh=mesh,
        in_specs=(placed, placed, placed, P(), P(), P(), P("seg")),
        out_specs=placed,
        check_vma=False,
    )
```

```python
import functools

import numpy as np
import jax
import jax.numpy as jnp
from jax import lax
from jax.experimental import pallas as pl
from jax.experimental.pallas import tpu as pltpu
from jax.sharding import PartitionSpec as P

TIME_STEP = 0.05
GAMMAS = (8.0 / 15.0, 5.0 / 12.0, 3.0 / 4.0)
ZETAS = (0.0, -17.0 / 60.0, -5.0 / 12.0)
SECTIONS = 3
WHOLE = (True, False)
GROUPS = ((0,), (1, 2))
TOP = 32767.0
STEPS_PER_OCTAVE = 64.0
F32 = jnp.float32
BF16 = jnp.bfloat16
VMEM_LIMIT = 60 * 1024 * 1024


def spectral_table(points):
    offset = np.arange(points)[:, None] - np.arange(points)[None, :]
    away = np.where(offset == 0, 1, offset)
    table = 0.5 * (1 - 2 * (offset % 2)) / np.tan(np.pi * away / points)
    return np.where(offset == 0, 0.0, table).astype(np.float32)


def halves(table):
    high = table.astype(jnp.bfloat16)
    low = (table - high.astype(np.float32)).astype(jnp.bfloat16)
    return np.asarray(high), np.asarray(low)


def split(value):
    high = value.astype(BF16)
    return high, (value - high.astype(F32)).astype(BF16)


def dot(left, right):
    return jnp.dot(left, right, preferred_element_type=F32)


def aligned(value, multiple):
    return value if isinstance(value, int) else pl.multiple_of(value, multiple)


def bits_of(parts):
    half = parts // 2
    far = list(range(half, parts))
    near = [d for d in range(1, half) if d != half // 2][::-1]
    return [0, half // 2, *far, *near] if parts > 2 else list(range(parts))


def partner(plan, whole, me, d):
    return d if whole else me ^ plan.bits[d]


class Plan:
    def __init__(self, rows, nx, nz, parts):
        self.rows, self.nx, self.nz, self.parts = rows, nx, nz, parts
        self.cuts = 1 if nx // parts >= 16 else 2
        self.width = nx * self.cuts // parts
        self.depth = nz // self.cuts
        self.lines = rows * parts
        self.bits = bits_of(parts)
        self.scale_rows = -(-rows // 16) * 16
        early = max(rows // 4, 1)
        self.early, self.late = early, rows - early

    def rows_of(self, fields, rows=None):
        return fields * (rows or self.rows) * self.width

    def piece(self, number):
        along = aligned(number // self.cuts * self.width, self.width)
        if self.cuts == 1:
            return pl.ds(along, self.width), pl.ds(0, self.depth)
        across = aligned(number % self.cuts * self.depth, self.depth)
        return pl.ds(along, self.width), pl.ds(across, self.depth)


def scale_code(largest):
    return jnp.floor(jnp.log2(jnp.maximum(largest, 1e-35)) * STEPS_PER_OCTAVE) + 2.0


def encode(code):
    return TOP * jnp.exp2(code * (-1.0 / STEPS_PER_OCTAVE))


def decode(code):
    return (1.0 / TOP) * jnp.exp2(code * (1.0 / STEPS_PER_OCTAVE))


def to_short(value):
    return jnp.round(value).astype(jnp.int32).astype(jnp.int16)


def from_short(value):
    return value.astype(jnp.int32).astype(F32)


def column_max(values):
    return functools.reduce(
        jnp.maximum, [jnp.max(jnp.abs(v), axis=0, keepdims=True) for v in values]
    )


def pack_kernel(plan, tangent_ref, flow_ref, out_ref, codes):
    step, size = pl.program_id(0), tangent_ref.shape[1]
    for j in range(size):
        row = step * size + j
        for d in range(plan.parts):
            along, across = plan.piece(d)
            values = [tangent_ref[c, j, along, across] for c in range(3)]
            values.append(flow_ref[0, j, along, across].astype(F32))
            for first, group in ((0, values[:3]), (3, values[3:])):
                code = scale_code(column_max(group))
                factor = encode(code)
                for k, value in enumerate(group):
                    start = ((first + k) * plan.rows + row) * plan.width
                    here = pl.ds(pl.multiple_of(start, plan.width), plan.width)
                    out_ref[d, here, :] = to_short(value * factor)
                base = 0 if first == 0 else plan.scale_rows
                codes[d, pl.ds(base + row, 1), :] = code

    @pl.when(step == pl.num_programs(0) - 1)
    def _():
        for d in range(plan.parts):
            out_ref[d, plan.rows_of(4) :, :] = codes[d].astype(jnp.int32).astype(jnp.int16)


def pack_start(plan, tangent, flow):
    shape = (plan.parts, plan.rows_of(4) + 2 * plan.scale_rows, plan.depth)
    size = 4 if plan.rows % 4 == 0 else 1
    return pl.pallas_call(
        functools.partial(pack_kernel, plan),
        grid=(plan.rows // size,),
        in_specs=[
            pl.BlockSpec((3, size, plan.nx, plan.nz), lambda j: (0, j, 0, 0)),
            pl.BlockSpec((1, size, plan.nx, plan.nz), lambda j: (1, j, 0, 0)),
        ],
        out_specs=pl.BlockSpec(shape, lambda j: (0, 0, 0)),
        scratch_shapes=[pltpu.VMEM((plan.parts, 2 * plan.scale_rows, plan.depth), F32)],
        out_shape=jax.ShapeDtypeStruct(shape, jnp.int16),
        compiler_params=pltpu.CompilerParams(vmem_limit_bytes=VMEM_LIMIT),
        cost_estimate=pl.CostEstimate(flops=0, transcendentals=0, bytes_accessed=20_000_000),
        name="pack_start",
    )(tangent, flow)


def pieces(plan, whole):
    return 1 if whole else plan.parts


def each(plan, whole, refs):
    return [refs[0].at[d] for d in range(plan.parts)] if whole else list(refs)


def block_specs(plan, whole, rows, depth, index, **more):
    if whole:
        return [pl.BlockSpec((plan.parts, rows, depth), lambda i, *_: (0, index(i), 0), **more)]
    return [pl.BlockSpec((rows, depth), lambda i, *_: (index(i), 0), **more)] * plan.parts


def block_shapes(plan, whole, rows):
    shape = (plan.parts, rows, plan.depth) if whole else (rows, plan.depth)
    return [jax.ShapeDtypeStruct(shape, jnp.int16)] * pieces(plan, whole)


def flat(groups):
    return [block for blocks in groups for block in blocks]


def grouped(plan, refs):
    lists = []
    for whole in WHOLE:
        count = pieces(plan, whole)
        lists.append(refs[:count])
        refs = refs[count:]
    return lists, refs


def receive(plan, me, row, sources, scales, speed):
    for whole, group, blocks, factors in zip(WHOLE, GROUPS, sources, scales):
        for d in range(plan.parts):
            along, across = plan.piece(partner(plan, whole, me, d))
            for k, c in enumerate(group):
                start = pl.multiple_of((k * plan.rows + row) * plan.width, plan.width)
                value = from_short(blocks[d][pl.ds(start, plan.width), :])
                speed[c, along, across] = value * factors[d, k : k + 1, :]


def prepare(plan, sources, scales):
    for group, blocks, factors in zip(GROUPS, sources, scales):
        for d in range(plan.parts):
            factors[d] = decode(from_short(blocks[d][plan.rows_of(len(group)) :, :]))


def blockwise(plan, refs):
    lists, rest = grouped(plan, refs)
    return [each(plan, whole, blocks) for whole, blocks in zip(WHOLE, lists)], rest


def explicit_kernel(plan, late, received, me_ref, *refs):
    parts, nx = plan.parts, plan.nx
    if received:
        sources, refs = blockwise(plan, refs)
    else:
        tangent_ref, refs = refs[0], refs[1:]
    flow_ref, shear_ref, dx_ref, dz_ref = refs[:4]
    refs = refs[4:]
    if received:
        base_dx_ref, base_dz_ref, refs = refs[0], refs[1], refs[2:]
    if late:
        above, rows, whole, groups = plan.early, plan.late, False, GROUPS
    else:
        above, rows, whole, groups = 0, plan.early, True, ((0, 1, 2),)
    outs = []
    for _ in groups:
        count = pieces(plan, whole)
        outs.append(each(plan, whole, refs[:count]))
        refs = refs[count:]
    if not received:
        base_dx_ref, base_dz_ref, refs = refs[0], refs[1], refs[2:]
    speed, term, codes = refs[:3]
    scales = refs[3:]
    row = pl.program_id(0)
    me = me_ref[0]
    if received:

        @pl.when(row == 0)
        def _():
            prepare(plan, sources, scales)

        receive(plan, me, above + row, sources, scales, speed)
    else:
        for c in range(3):
            speed[c] = tangent_ref[c, 0]
    for c in range(3):
        if not received:
            flow = flow_ref[c, 0]
            both = dot(dx_ref[...], flow)
            base_dx_ref[c, 0] = both[:nx] + both[nx:]
            base_dz_ref[c, 0] = dot(flow, dz_ref[0]) + dot(flow, dz_ref[1])
        high, low = split(speed[c])
        both = dot(dx_ref[...], high)
        along_x = both[:nx] + both[nx:] + dot(dx_ref[:nx, :], low)
        along_z = dot(high, dz_ref[0]) + (dot(low, dz_ref[0]) + dot(high, dz_ref[1]))
        carried = flow_ref[0, 0].astype(F32) * along_x + flow_ref[2, 0].astype(F32) * along_z
        sheared = (
            speed[0] * base_dx_ref[c, 0]
            + speed[1] * shear_ref[c, 0].astype(F32)
            + speed[2] * base_dz_ref[c, 0]
        )
        term[c] = -(carried + sheared)
    for d in range(parts):
        along, across = plan.piece(partner(plan, whole, me, d))
        values = [term[c, along, across] for c in range(3)]
        code = scale_code(column_max(values))
        factor = encode(code)
        for group, blocks in zip(groups, outs):
            for k, c in enumerate(group):
                start = pl.multiple_of((k * rows + row) * plan.width, plan.width)
                blocks[d][pl.ds(start, plan.width), :] = to_short(values[c] * factor)
        codes[d, pl.ds(row, 1), :] = code

    @pl.when(row == rows - 1)
    def _():
        for d in range(parts):
            shorts = codes[d].astype(jnp.int32).astype(jnp.int16)
            outs[0][d][plan.rows_of(len(groups[0]), rows) :, :] = shorts


def whole_blocks(plan):
    specs = []
    for whole, group in zip(WHOLE, GROUPS):
        height = plan.rows_of(len(group)) + 16
        once = dict(pipeline_mode=pl.Buffered(1))
        specs += block_specs(plan, whole, height, plan.depth, lambda j: 0, **once)
    return specs


def explicit(plan, late, me, velocity, flow, shear, dx, dz, bases=None):
    received = bases is not None
    parts = plan.parts
    if late:
        above, rows, whole = plan.early, plan.late, False
        heights = [plan.rows_of(len(group), rows) for group in GROUPS]
    else:
        above, rows, whole, heights = 0, plan.early, True, [plan.rows_of(3, plan.early)]
    heights[0] += plan.scale_rows
    block = (3, 1, plan.nx, plan.nz)
    field = pl.BlockSpec(block, lambda j, *_: (0, above + j, 0, 0))
    own = pl.BlockSpec(block, lambda j, *_: (0, j, 0, 0))
    scratch = [
        pltpu.VMEM((3, plan.nx, plan.nz), F32),
        pltpu.VMEM((3, plan.nx, plan.nz), F32),
        pltpu.VMEM((parts, plan.scale_rows, plan.depth), F32),
    ]
    out_specs, out_shape = [], []
    for height in heights:
        out_specs += block_specs(plan, whole, height, plan.depth, lambda j: 0)
        out_shape += block_shapes(plan, whole, height)
    if received:
        first, more = whole_blocks(plan), [own, own]
        velocity = flat(velocity)
        scratch += [pltpu.VMEM((parts, 16, plan.depth), F32)] * len(GROUPS)
    else:
        first, velocity, bases, more = [field], [velocity], [], []
        out_specs += [own, own]
        out_shape += [jax.ShapeDtypeStruct((3, rows, plan.nx, plan.nz), F32)] * 2
    results = pl.pallas_call(
        functools.partial(explicit_kernel, plan, late, received),
        grid_spec=pltpu.PrefetchScalarGridSpec(
            num_scalar_prefetch=1,
            grid=(rows,),
            in_specs=first
            + [
                field,
                field,
                pl.BlockSpec(dx.shape, lambda j, *_: (0, 0)),
                pl.BlockSpec(dz.shape, lambda j, *_: (0, 0, 0)),
            ]
            + more,
            out_specs=out_specs,
            scratch_shapes=scratch,
        ),
        out_shape=out_shape,
        compiler_params=pltpu.CompilerParams(vmem_limit_bytes=VMEM_LIMIT),
        cost_estimate=pl.CostEstimate(
            flops=1_000_000_000 * rows, transcendentals=0, bytes_accessed=4_000_000 * rows
        ),
        name="explicit",
    )(me, *velocity, flow, shear, dx, dz, *bases)
    count = pieces(plan, whole)
    blocks = [list(results[i * count : (i + 1) * count]) for i in range(len(heights))]
    return blocks, results[count * len(heights) :]


def stacked(matrices):
    rows = []
    for matrix in matrices:
        high, low = split(matrix)
        rows.append(jnp.concatenate([high, high], axis=1))
        rows.append(jnp.concatenate([low, jnp.zeros_like(low)], axis=1))
    return jnp.concatenate(rows, axis=0)


def precise_dot(left, right):
    high, low = split(left)
    right_high, right_low = split(right)
    return dot(high, right_high) + (dot(low, right_high) + dot(high, right_low))


def put(field, rows, value):
    for half in range(field.shape[0]):
        field[half, rows, :] = value[:, half * 128 : half * 128 + 128]


def get(field, rows):
    return jnp.concatenate([field[half, rows, :] for half in range(field.shape[0])], axis=1)


def unpack_lines(plan, whole, me, span, sources, scales, field):
    above, rows = span
    for d, (source, scale) in enumerate(zip(sources, scales)):
        scale = decode(from_short(scale[...]))
        first = aligned(partner(plan, whole, me, d) * plan.rows_of(1), plan.width)
        for j in range(rows):
            value = from_short(source[j * plan.width : (j + 1) * plan.width, :])
            here = pl.ds(first + (above + j) * plan.width, plan.width)
            put(field, here, value * scale[j : j + 1, :])


def first_lines_kernel(plan, *refs):
    lines = plan.lines
    values, scales, flows, flow_scales = (each(plan, True, refs[i : i + 1]) for i in range(4))
    wall_ref, right_ref, turned_ref, flow_ref, field, table = refs[4:]

    @pl.when(pl.program_id(0) == 0)
    def _():
        table[...] = stacked([wall_ref[...]])
        unpack_lines(plan, True, None, (0, plan.rows), flows, flow_scales, field)

        def turn(r, carry):
            flow_ref[r] = get(field, pl.ds(r, lines, stride=plan.width))
            return carry

        lax.fori_loop(0, plan.width, turn, 0)

    unpack_lines(plan, True, None, (0, plan.rows), values, scales, field)

    def line(r, carry):
        value = get(field, pl.ds(r, lines, stride=plan.width))
        product = dot(table[...], jnp.concatenate(split(value), axis=0))
        turned = -(flow_ref[r] * (product[:lines] + product[lines:]))
        turned_ref[0, r] = turned
        right_ref[0, r] = value + (TIME_STEP * GAMMAS[0]) * turned
        return carry

    lax.fori_loop(0, plan.width, line, 0, unroll=4)


def first_lines(plan, blocks, wall):
    lines, width, depth = plan.lines, plan.width, plan.depth
    at = plan.rows_of(4) // plan.scale_rows
    rows, codes = plan.rows_of(1), plan.scale_rows
    state = jax.ShapeDtypeStruct((3, width, lines, depth), F32)
    state_spec = pl.BlockSpec((1, width, lines, depth), lambda c: (c, 0, 0, 0))
    return pl.pallas_call(
        functools.partial(first_lines_kernel, plan),
        grid=(3,),
        in_specs=block_specs(plan, True, rows, depth, lambda c: c)
        + block_specs(plan, True, codes, depth, lambda c: at)
        + block_specs(plan, True, rows, depth, lambda c: 3)
        + block_specs(plan, True, codes, depth, lambda c: at + 1)
        + [pl.BlockSpec(wall.shape, lambda c: (0, 0))],
        out_specs=[
            state_spec,
            state_spec,
            pl.BlockSpec((width, lines, depth), lambda c: (0, 0, 0)),
        ],
        scratch_shapes=[
            pltpu.VMEM((depth // 128, lines * width, 128), F32),
            pltpu.VMEM((2 * lines, 2 * lines), BF16),
        ],
        out_shape=[state, state, jax.ShapeDtypeStruct((width, lines, depth), F32)],
        compiler_params=pltpu.CompilerParams(vmem_limit_bytes=VMEM_LIMIT),
        cost_estimate=pl.CostEstimate(
            flops=1_000_000_000, transcendentals=0, bytes_accessed=30_000_000
        ),
        name="first_lines",
    )(blocks, blocks, blocks, blocks, wall)


def lines_kernel(plan, section, group, whole, me_ref, *refs):
    parts, lines = plan.parts, plan.lines
    last = section == SECTIONS - 1
    count = pieces(plan, whole)
    values, refs = blockwise(plan, refs)
    scales, refs = blockwise(plan, refs)
    if last:
        wall_ref, solve_ref, right_ref = refs[:3]
        outs, (field, table, codes) = refs[3 : 3 + count], refs[3 + count :]
    else:
        wall_ref, solve_ref, right_ref, turned_ref, flow_ref = refs[:5]
        outs, refs = refs[5 : 5 + count], refs[5 + count :]
        right_out, turned_out, field, table, codes = refs
    outs = each(plan, whole, outs)
    me = me_ref[0]
    component = pl.program_id(0)

    @pl.when(component == 0)
    def _():
        solve = solve_ref[0]
        tables = [solve] if last else [solve, precise_dot(wall_ref[...], solve)]
        table[...] = stacked(tables)
        codes[...] = jnp.zeros_like(codes)

    spans = ((0, plan.early), (plan.early, plan.late))
    for kind, span, blocks, codings in zip((True, False), spans, values, scales):
        unpack_lines(plan, kind, me, span, blocks, codings, field)

    def line(r, carry):
        here = pl.ds(r, lines, stride=plan.width)
        term = get(field, here)
        right = right_ref[0, r] + (TIME_STEP * GAMMAS[section]) * term
        product = dot(table[...], jnp.concatenate(split(right), axis=0))
        value = product[:lines] + product[lines : 2 * lines]
        put(field, here, value)
        if not last:
            slope = product[2 * lines : 3 * lines] + product[3 * lines :]
            turned = -(flow_ref[r] * slope)
            past = term + turned_ref[0, r]
            turned_out[0, r] = turned
            right_out[0, r] = (
                value
                + (TIME_STEP * ZETAS[section + 1]) * past
                + (TIME_STEP * GAMMAS[section + 1]) * turned
            )
        return carry

    lax.fori_loop(0, plan.width, line, 0, unroll=4)

    for d in range(parts):
        first = aligned(partner(plan, whole, me, d) * plan.rows_of(1), plan.width)
        chunk = [
            get(field, pl.ds(first + j * plan.width, plan.width)) for j in range(plan.rows)
        ]
        code = scale_code(column_max(chunk))
        factor = encode(code)
        for j in range(plan.rows):
            start = pl.multiple_of((component * plan.rows + j) * plan.width, plan.width)
            outs[d][pl.ds(start, plan.width), :] = to_short(chunk[j] * factor)
        codes[d, pl.ds(component, 1), :] = code

    @pl.when(component == len(group) - 1)
    def _():
        for d in range(parts):
            outs[d][plan.rows_of(len(group)) :, :] = codes[d].astype(jnp.int32).astype(jnp.int16)


def advance_lines(plan, section, group, whole, me, blocks, wall, solves, right, turned, flow):
    lines, width, depth = plan.lines, plan.width, plan.depth
    last = section == SECTIONS - 1
    height = plan.rows_of(len(group)) + 16
    skip = group[0] if right.shape[0] == 3 else 0
    early, first_late, late = blocks
    early_at = plan.rows_of(3, plan.early) // plan.scale_rows
    late_at = plan.rows_of(len(GROUPS[0]), plan.late) // plan.scale_rows
    rows = plan.rows_of(1, plan.early), plan.rows_of(1, plan.late)
    value_specs = block_specs(plan, True, rows[0], depth, lambda c: c + group[0])
    value_specs += block_specs(plan, False, rows[1], depth, lambda c: c)
    scale_specs = block_specs(plan, True, plan.scale_rows, depth, lambda c: early_at)
    scale_specs += block_specs(plan, False, plan.scale_rows, depth, lambda c: late_at)
    state_spec = pl.BlockSpec((1, width, lines, depth), lambda c, *_: (c, 0, 0, 0))
    read_spec = pl.BlockSpec((1, width, lines, depth), lambda c, *_: (c + skip, 0, 0, 0))
    in_specs = (
        value_specs
        + scale_specs
        + [
            pl.BlockSpec(wall.shape, lambda c, *_: (0, 0)),
            pl.BlockSpec((1, lines, lines), lambda c, *_: (section, 0, 0)),
            read_spec,
        ]
    )
    args = [me, *early, *late, *early, *first_late, wall, solves, right]
    out_specs = block_specs(plan, whole, height, depth, lambda c: 0)
    out_shape = block_shapes(plan, whole, height)
    copies = 2
    if not last:
        in_specs += [
            read_spec,
            pl.BlockSpec(flow.shape, lambda c, *_: (0, 0, 0), pipeline_mode=pl.Buffered(1)),
        ]
        args += [turned, flow]
        out_specs = out_specs + [state_spec, state_spec]
        state = jax.ShapeDtypeStruct((len(group), width, lines, depth), F32)
        out_shape = out_shape + [state, state]
        copies = 4
    results = pl.pallas_call(
        functools.partial(lines_kernel, plan, section, group, whole),
        grid_spec=pltpu.PrefetchScalarGridSpec(
            num_scalar_prefetch=1,
            grid=(len(group),),
            in_specs=in_specs,
            out_specs=out_specs,
            scratch_shapes=[
                pltpu.VMEM((depth // 128, lines * width, 128), F32),
                pltpu.VMEM((copies * lines, 2 * lines), BF16),
                pltpu.VMEM((plan.parts, 16, depth), F32),
            ],
        ),
        out_shape=out_shape,
        compiler_params=pltpu.CompilerParams(vmem_limit_bytes=VMEM_LIMIT),
        cost_estimate=pl.CostEstimate(
            flops=700_000_000 * len(group),
            transcendentals=0,
            bytes_accessed=17_000_000 * len(group),
        ),
        name="advance_lines",
    )(*args)
    count = pieces(plan, whole)
    return results[:count], results[count:]


def result_kernel(plan, group, whole, me_ref, shift_ref, successor_ref, *refs):
    count = pieces(plan, whole)
    blocks, refs = each(plan, whole, refs[:count]), refs[count:]
    follower_ref, (out_ref, speed, factors) = refs[0], refs[-3:]
    component, step = pl.program_id(0), pl.program_id(1)

    @pl.when((component == 0) & (step == 0))
    def _():
        for d in range(plan.parts):
            factors[d] = decode(from_short(blocks[d][plan.rows_of(len(group)) :, :]))

    rows = out_ref.shape[1]
    for j in range(rows):
        row = component * plan.rows + step * rows + j
        for d in range(plan.parts):
            along, across = plan.piece(partner(plan, whole, me_ref[0], d))
            start = pl.multiple_of(row * plan.width, plan.width)
            value = from_short(blocks[d][pl.ds(start, plan.width), :])
            speed[j, along, across] = value * factors[d, pl.ds(component, 1), :]
        rolled = pltpu.roll(speed[j], shift_ref[0], axis=1)
        out_ref[0, j] = rolled - follower_ref[0, 0, j]


def result(plan, group, whole, me, shift, successor, blocks, tangents, before):
    height = plan.rows_of(len(group)) + 16
    rows = next(r for r in (6, 4, 3, 2, 1) if plan.rows % r == 0)
    specs = block_specs(
        plan, whole, height, plan.depth, lambda c: 0, pipeline_mode=pl.Buffered(1)
    )
    specs.append(
        pl.BlockSpec(
            (1, 1, rows, plan.nx, plan.nz),
            lambda c, j, me, shift, successor: (successor[0], c + group[0], j, 0, 0),
        )
    )
    args = [me, shift, successor, *blocks, tangents]
    aliases = {}
    if before is not None:
        specs.append(pl.BlockSpec(memory_space=pl.ANY))
        aliases[len(args)] = 0
        args.append(before)
    return pl.pallas_call(
        functools.partial(result_kernel, plan, group, whole),
        grid_spec=pltpu.PrefetchScalarGridSpec(
            num_scalar_prefetch=3,
            grid=(len(group), plan.rows // rows),
            in_specs=specs,
            out_specs=pl.BlockSpec(
                (1, rows, plan.nx, plan.nz), lambda c, j, *_: (c + group[0], j, 0, 0)
            ),
            scratch_shapes=[
                pltpu.VMEM((rows, plan.nx, plan.nz), F32),
                pltpu.VMEM((plan.parts, 16, plan.depth), F32),
            ],
        ),
        out_shape=jax.ShapeDtypeStruct((3, plan.rows, plan.nx, plan.nz), F32),
        input_output_aliases=aliases,
        compiler_params=pltpu.CompilerParams(vmem_limit_bytes=VMEM_LIMIT),
        cost_estimate=pl.CostEstimate(
            flops=0, transcendentals=0, bytes_accessed=8_000_000 * len(group)
        ),
        name="result",
    )(*args)


def exchange(plan, whole, blocks):
    if whole:
        return [lax.all_to_all(blocks[0], "grid", split_axis=0, concat_axis=0, tiled=True)]
    moved = list(blocks)
    for d in range(1, plan.parts):
        route = [(i, i ^ plan.bits[d]) for i in range(plan.parts)]
        moved[d] = lax.ppermute(blocks[d], "grid", route)
    return moved


def shards(
    tangent, base_flow, base_shear, wall_derivative, implicit_inverse, successor, spanwise_shift
):
    tangent, flow, shear = tangent[0], base_flow[0], base_shear[0]
    _, rows, nx, nz = tangent.shape
    plan = Plan(rows, nx, nz, lax.axis_size("grid"))
    me = lax.axis_index("grid").astype(jnp.int32).reshape(1)
    ahead = lax.dynamic_slice_in_dim(successor, lax.axis_index("seg"), 1)
    dx = jnp.asarray(np.concatenate(halves(spectral_table(nx)), axis=0))
    dz = jnp.asarray(np.stack(halves(spectral_table(nz).T)))

    start = pack_start(plan, tangent, flow)
    later, start, following = lax.optimization_barrier((me, start, tangent))
    tangents = lax.all_gather(following, "seg")
    (start,) = exchange(plan, True, [start])
    bases = []
    early, base = explicit(plan, False, later, tangent, flow, shear, dx, dz)
    bases.append(base)
    late, base = explicit(plan, True, later, tangent, flow, shear, dx, dz)
    bases.append(base)
    right, turned, wall_flow = first_lines(plan, start, wall_derivative)
    early[0][0], late = lax.optimization_barrier((early[0][0], late))
    early = exchange(plan, True, early[0])
    late, wall_flow = lax.optimization_barrier((late, wall_flow))
    term = [early, [exchange(plan, False, blocks) for blocks in late]]
    states = [(right, turned) for _ in GROUPS]
    for section in range(SECTIONS):
        value = []
        for g, (whole, group) in enumerate(zip(WHOLE, GROUPS)):
            blocks, states[g] = advance_lines(
                plan,
                section,
                group,
                whole,
                me,
                [term[0], term[1][0], term[1][g]],
                wall_derivative,
                implicit_inverse,
                *(states[g] if section < SECTIONS - 1 else (states[g][0], None)),
                wall_flow,
            )
            if g == 0:
                blocks, term[1][1] = lax.optimization_barrier((blocks, term[1][1]))
            value.append(exchange(plan, whole, blocks))
        if section < SECTIONS - 1:
            early, _ = explicit(plan, False, me, value, flow, shear, dx, dz, bases[0])
            early = exchange(plan, True, early[0])
            late, _ = explicit(plan, True, me, value, flow, shear, dx, dz, bases[1])
            term = [early, [exchange(plan, False, blocks) for blocks in late]]
    out = None
    for group, whole, blocks in zip(GROUPS, WHOLE, value):
        out = result(plan, group, whole, me, spanwise_shift, ahead, blocks, tangents, out)
    return out[None]


def solution(mesh):
    placed = P("seg", None, "grid", None, None)
    return jax.shard_map(
        shards,
        mesh=mesh,
        in_specs=(placed, placed, placed, P(), P(), P(), P("seg")),
        out_specs=placed,
        check_vma=False,
    )
```
